128 devices in a mesh: depth: 4 (over x_lo, core), height: 32 (over x_hi, z, y).
Axes of the slice: x: 4 (x_hi: 2, x_lo: 2; x = x_hi * 2 + x_lo), y: 4, z: 4, core: 2. Of those that a mesh axis runs over, the one named last changes fastest.
Arguments:
- fixed_image: float32 [32, 128, 128], P('depth', 'height'), as said below
- moving_image: float32 [32, 128, 128], P('depth', 'height'), as said below
- conv_one: float32 [64, 1, 3, 3, 3], replicated, may hold values from -1.25 to 1.25
- gain_one: float32 [64], replicated, may hold values from 0.1 to 1.9
- shift_one: float32 [64], replicated, may hold values from -3 to 3
- conv_two: bfloat16 [27, 4096], replicated, may hold values from -0.15625 to 0.15625
- gain_two: float32 [64], replicated, may hold values from 0.1 to 1.9
- shift_two: float32 [64], replicated, may hold values from -3 to 3
- sharpness: float32 [1], replicated, may hold values from 1 to 4
Outputs:
- displacement: float32 [3, 32, 128, 128], P(None, 'depth', 'height')
The draws below stay inside these ranges and needn't reach their ends.
Inputs may be any that keep to these rules, and one draw needn't show every extreme that they name: `fixed_image`: intensities of a scan; the two scans show the same anatomy. `moving_image`: intensities of a scan; the two scans show the same anatomy.
All inputs are finite; a program needn't handle non-finite values.
Results may differ from the reference program's by a relative error of at most 0.0049.
Values may be sent and summed in bfloat16 or wider, within the bound.
A program may use at most 64 MiB of HBM per device.

```python
import math
import jax
import jax.numpy as jnp
from jax import lax

C = 64
RADIUS = 3
WIDTH = 128
DEPTH = 32
HEIGHT = 128


def base_volume(key):
    noise = jax.random.normal(jax.random.fold_in(key, 17), (DEPTH, HEIGHT, WIDTH), jnp.float32)
    depth_pos = jnp.arange(DEPTH, dtype=jnp.float32) / DEPTH
    height_pos = jnp.arange(HEIGHT, dtype=jnp.float32) / HEIGHT
    across = jnp.ones((WIDTH,), jnp.float32)
    envelope = jnp.exp(jnp.log(3.0) * (depth_pos[:, None, None] + height_pos[None, :, None])) * across[None, None, :]
    return (noise, envelope)


def draw_fixed_image(key, part):
    noise, envelope = base_volume(key)
    return noise * envelope


def draw_moving_image(key, part):
    noise, envelope = base_volume(key)
    moved = jnp.roll(noise, (1, -2, 1), axis=(0, 1, 2))
    jitter = 0.3 * jax.random.normal(jax.random.fold_in(key, 29), (DEPTH, HEIGHT, WIDTH), jnp.float32)
    return (moved + jitter) * envelope


def scatter_about(stream_key, shape, width, reach, kind=jnp.bfloat16):
    entries = jax.random.normal(stream_key, shape, jnp.float32) * width
    return jnp.minimum(jnp.maximum(entries, -reach), reach).astype(kind)


def setup_inputs(seed: int = 0) -> dict:
    seeds = jax.random.split(jax.random.key(seed), 10)
    return {
        "fixed_image": draw_fixed_image(jax.random.fold_in(seeds[9], 71), 0),
        "moving_image": draw_moving_image(jax.random.fold_in(seeds[9], 71), 0),
        "conv_one": scatter_about(seeds[2], (C, 1, 3, 3, 3), 27 ** -0.5, 1.25, jnp.float32),
        "gain_one": jnp.clip(1.0 + 0.18 * jax.random.normal(seeds[3], (C,), jnp.float32), 0.1, 1.9),
        "shift_one": scatter_about(seeds[4], (C,), 0.5, 3.0, jnp.float32),
        "conv_two": scatter_about(seeds[5], (27, C * C), (27 * C) ** -0.5, 0.15625),
        "gain_two": jnp.clip(1.0 + 0.18 * jax.random.normal(seeds[6], (C,), jnp.float32), 0.1, 1.9),
        "shift_two": scatter_about(seeds[7], (C,), 0.5, 3.0, jnp.float32),
        "sharpness": jnp.clip(jnp.exp(jax.random.uniform(seeds[8], (1,), jnp.float32, math.log(1.0), math.log(4.0))), 1.0, 4.0),
    }


def convolve(field, kernel):
    return lax.conv_general_dilated(field, kernel, (1, 1, 1), [(1, 1), (1, 1), (1, 1)], dimension_numbers=('NCDHW', 'OIDHW', 'NCDHW'), precision=lax.Precision.HIGHEST)

def kernel_two(flat_kernel):
    return jnp.transpose(flat_kernel.reshape(3, 3, 3, C, C), (4, 3, 0, 1, 2))

def instance_norm(raw, gain, shift):
    mean_val = lax.optimization_barrier(jnp.mean(raw, axis=(2, 3, 4), keepdims=True))
    mean_sq = lax.optimization_barrier(jnp.mean(raw * raw, axis=(2, 3, 4), keepdims=True))
    scaled = (raw - mean_val) * lax.rsqrt(mean_sq - mean_val * mean_val + 1e-05)
    scaled = scaled * gain[None, :, None, None, None] + shift[None, :, None, None, None]
    return jax.nn.leaky_relu(scaled, 0.01).astype(jnp.bfloat16)

def reference(fixed_image, moving_image, conv_one, gain_one, shift_one, conv_two, gain_two, shift_two, sharpness):
    both_images = jnp.stack([fixed_image, moving_image])[:, None].astype(jnp.float32)
    first_raw = convolve(both_images, conv_one.astype(jnp.float32))
    first_feat = instance_norm(first_raw, gain_one, shift_one)
    second_raw = convolve(first_feat.astype(jnp.float32), kernel_two(conv_two).astype(jnp.float32))
    features = instance_norm(second_raw, gain_two, shift_two)
    fixed_feat = features[0].astype(jnp.float32)
    padded = jnp.pad(features[1], ((0, 0), (RADIUS, RADIUS), (RADIUS, RADIUS), (RADIUS, RADIUS)))
    span = 2 * RADIUS + 1
    factor = sharpness[0] / C

    def step(state, offset):
        running_max, running_sum, running_vec = state
        depth_shift = (offset // (span * span)).astype(jnp.int32)
        height_shift = (offset // span % span).astype(jnp.int32)
        width_shift = (offset % span).astype(jnp.int32)
        window = lax.dynamic_slice(padded, (jnp.int32(0), depth_shift, height_shift, width_shift), (C, DEPTH, HEIGHT, WIDTH))
        difference = fixed_feat - window.astype(jnp.float32)
        scores = -factor * lax.optimization_barrier(jnp.sum(difference * difference, axis=0))
        new_max = jnp.maximum(running_max, scores)
        keep = jnp.exp(running_max - new_max)
        weights = jnp.exp(scores - new_max)
        vector = jnp.stack([depth_shift, height_shift, width_shift]).astype(jnp.float32) - RADIUS
        running_sum = running_sum * keep + weights
        running_vec = running_vec * keep[None] + weights[None] * vector[:, None, None, None]
        return ((new_max, running_sum, running_vec), None)
    start = (jnp.full((DEPTH, HEIGHT, WIDTH), -jnp.inf, jnp.float32), jnp.zeros((DEPTH, HEIGHT, WIDTH), jnp.float32), jnp.zeros((3, DEPTH, HEIGHT, WIDTH), jnp.float32))
    final, _ = lax.scan(step, start, jnp.arange(span * span * span, dtype=jnp.int32))
    return final[2] / final[1][None]
```

```python
import math

import jax
import jax.numpy as jnp
from jax import lax
from jax.experimental import pallas as pl
from jax.experimental.pallas import tpu as pltpu
from jax.sharding import PartitionSpec as P

MESH = pl.DeviceIdType.MESH
F32, BF16, I32 = jnp.float32, jnp.bfloat16, jnp.int32
BIG = 1e30
CELLS = 32 * 128 * 128
HALO = [(dd, hh) for hh in (-2, -1, 0, 1, 2) for dd in (-1, 0, 1) if (dd, hh) != (0, 0)]
HEIGHT_SPAN = {0: (0, 4, 5), 1: (0, 4, 1), 2: (3, 4, 0), -1: (0, 4, 9), -2: (0, 1, 13)}


def iota(shape, dim):
    return lax.broadcasted_iota(I32, shape, dim)


def dot(a, b):
    return jnp.dot(a, b, preferred_element_type=F32)


def dot_nt(a, b):
    return lax.dot_general(a, b, (((1,), (1,)), ((), ())), preferred_element_type=F32)


def rows_sum(x):
    return jnp.sum(x.reshape(x.shape[0] // 8, 8, x.shape[1]), axis=0)


def position():
    depth, height = lax.axis_index("depth"), lax.axis_index("height")
    return depth, height


def group_peers(depth, height):
    x_hi, z, y = height // 16, (height // 4) % 4, height % 4
    along_x, along_y, along_z = [], [], []
    for k in range(1, 8):
        g = (x_hi * 4 + depth + k) % 8
        along_x.append((g % 4, (g // 4) * 16 + z * 4 + y))
    for k in range(1, 4):
        along_y.append((depth, x_hi * 16 + z * 4 + (y + k) % 4))
        along_z.append((depth, x_hi * 16 + ((z + k) % 4) * 4 + y))
    return along_x, along_y, along_z


def halo_peers(depth, height):
    return [((depth + dd + 4) % 4, (height + hh + 32) % 32) for dd, hh in HALO]


def total_over_devices(value, peers, bufs, send_sems, recv_sems, works):
    count = 0
    for group, buf, work in zip(peers, bufs, works):
        buf[0] = value
        copies = []
        for k, peer in enumerate(group):
            copy = pltpu.make_async_remote_copy(
                src_ref=buf.at[0],
                dst_ref=buf.at[k + 1],
                send_sem=send_sems.at[count],
                recv_sem=recv_sems.at[count],
                device_id=peer,
                device_id_type=MESH,
            )
            copy.start()
            copies.append(copy)
            count += 1
        work()
        for copy in copies:
            copy.wait()
        value = jnp.sum(buf[...], axis=0)
    return value


def leaky(v):
    return jnp.maximum(v, 0.01 * v)


def kernel(
    fi, mi, c1, g1, s1, c2, g2, s2, sharp,
    out,
    own, ext, selm, wf, wbig, w1, v, vs, raw1f, raw1m, wmask, xf, xm,
    raw2f, raw2m, ff, kf, kb, ke, qe, sbuf, res,
    ax1, ay1, az1, ax2, ay2, az2,
    hs, hr, as1, ar1, as2, ar2,
):
    depth, height = position()
    halo = halo_peers(depth, height)
    peers = group_peers(depth, height)

    barrier = pltpu.get_barrier_semaphore()
    everyone = halo + peers[0] + peers[1] + peers[2]
    for peer in everyone:
        pl.semaphore_signal(barrier, inc=1, device_id=peer, device_id_type=MESH)
    for h in range(4):
        own[h, 0] = fi[:, h, :]
        own[h, 1] = mi[:, h, :]
    k_i, n_i = iota((512, 1024), 0), iota((512, 1024), 1)
    hit = jnp.logical_and(
        k_i // 128 == (n_i // 32) % 4, k_i % 128 == 4 * (n_i % 32) - 2 + n_i // 128
    )
    selm[...] = jnp.where(hit, 1.0, 0.0).astype(BF16)
    pl.semaphore_wait(barrier, len(everyone))

    copies = []
    for n, (dd, hh) in enumerate(HALO):
        h0, h1, land = HEIGHT_SPAN[hh]
        block = 8 - 8 * dd
        copy = pltpu.make_async_remote_copy(
            src_ref=own.at[pl.ds(h0, h1 - h0)],
            dst_ref=ext.at[pl.ds(land, h1 - h0), :, pl.ds(block, 8), :],
            send_sem=hs.at[n],
            recv_sem=hr.at[n],
            device_id=halo[n],
            device_id_type=MESH,
        )
        copy.start()
        copies.append(copy)

    ext[5:9, :, 8:16, :] = own[...]
    for pair in range(32):
        wf[pl.ds(pair, 27, stride=32), :] = c2[:, pair * 128 : (pair + 1) * 128].astype(F32)

    def build(ab, carry):
        zero = jnp.zeros((64, 64), F32)
        taps = []
        for c in range(3):
            t = wf[pl.ds(pl.multiple_of((ab * 3 + c) * 32, 32), 32), :]
            taps.append(jnp.concatenate([t[:, :64], t[:, 64:]], axis=0))
        for u in range(6):
            parts = [taps[u - wo] if 0 <= u - wo <= 2 else zero for wo in range(4)]
            row = jnp.concatenate(parts, axis=1).astype(BF16)
            wbig[pl.ds(pl.multiple_of((ab * 6 + u) * 64, 64), 64), :] = row
        return carry

    lax.fori_loop(0, 9, build, 0)

    c1p = jnp.concatenate([c1[pl.ds(0, 32, stride=2), :], c1[pl.ds(1, 32, stride=2), :]], axis=0)
    c1t = jnp.transpose(c1p)
    c1t = c1t[:32]
    zero = jnp.zeros((32, 64), F32)
    spread = jnp.concatenate(
        [jnp.concatenate([c1t if q == u else zero for q in range(6)], axis=1) for u in range(6)],
        axis=0,
    )
    spread_hi = spread.astype(BF16)
    spread_lo = (spread - spread_hi.astype(F32)).astype(BF16)
    r_i, k_i = iota((72, 192), 0), iota((72, 192), 1)
    tap = k_i % 32
    hit = jnp.logical_and(
        tap // 3 == ((r_i // 8) % 3) * 3 + r_i // 24,
        jnp.logical_and(r_i % 8 - k_i // 32 == tap % 3, tap < 27),
    )
    pick = jnp.where(hit, 1.0, 0.0).astype(BF16)
    w1_hi, w1_lo = dot(pick, spread_hi), dot(pick, spread_lo)
    w1[...] = jnp.concatenate([w1_hi, w1_hi, w1_lo], axis=0).astype(BF16)

    row, lane = iota((384, 128), 0), iota((384, 128), 1)
    gh = height * 4 - 4 + row // 32
    inside = jnp.logical_and(gh >= 0, gh < 128)
    wmask[0] = jnp.where(
        jnp.logical_and(inside, jnp.logical_or(row % 32 > 0, lane >= 64)), 1.0, 0.0
    )
    wmask[1] = jnp.where(inside, 1.0, 0.0)
    wmask[2] = jnp.where(
        jnp.logical_and(inside, jnp.logical_or(row % 32 < 31, lane < 64)), 1.0, 0.0
    )
    q_i, lane = iota((256, 128), 0), iota((256, 128), 1)
    w_q = 4 * ((q_i // 32) % 2) + q_i // 64
    for odd in range(2):
        for phase in range(4):
            w_k = 4 * ((lane - 24 - 2 * odd + 8) % 4 - 1) + phase
            far = jnp.abs(w_k - w_q) > 3
            e = jnp.where(jnp.logical_and(lane < 12, lane // 3 == phase), -1.0, 0.0)
            e = jnp.where(lane - 12 == (q_i // 4) % 8, 1.0, e)
            e = jnp.where(jnp.logical_and(lane >= 20, lane - 20 == q_i % 4), 1.0, e)
            in_quad = jnp.logical_and(lane >= 24, lane < 28)
            e = jnp.where(jnp.logical_and(in_quad, far), -BIG, e)
            qe[odd, phase] = e.astype(BF16)
    kf[...] = jnp.zeros_like(kf)

    for copy in copies:
        copy.wait()

    row = iota((48, 128), 0)
    gd = depth * 8 - 8 + row % 24
    d_in = jnp.logical_and(gd >= 0, gd < 32)
    stacks = []
    for h4 in range(4):
        parts = []
        for hh in range(4):
            hx = h4 * 4 + hh
            if hx >= 14:
                parts.append(jnp.zeros((96, 128), BF16))
                continue
            x = ext[hx].reshape(48, 128)
            gh = jnp.full((48, 128), height * 4 - 5 + hx, I32)
            ok = jnp.logical_and(d_in, jnp.logical_and(gh >= 0, gh < 128))
            x = jnp.where(ok, x, 0.0)
            hi = x.astype(BF16)
            lo = (x - hi.astype(F32)).astype(BF16)
            parts.append(jnp.concatenate([hi, lo], axis=0))
        stacks.append(jnp.concatenate(parts, axis=1))
    for h4 in range(4):
        picked = dot(stacks[h4], selm[...])
        for q in range(4):
            for j in range(8):
                v[q, h4, pl.ds(j, 24, stride=8), :] = picked[
                    q * 24 : q * 24 + 24, j * 128 : (j + 1) * 128
                ]
    for q in range(4):
        full = jnp.concatenate([v[q, h4] for h4 in range(4)], axis=1)
        for b in range(3):
            vs[b, q] = full[:, 32 * b : 32 * b + 384]

    def patches(image, dx, lane0, lanes):
        start = pl.multiple_of((dx + 3) * 8, 8)
        parts = [
            vs[b, hl * 2 + image, pl.ds(start, 24), lane0 : lane0 + lanes]
            for hl in (0, 1, 0)
            for b in range(3)
        ]
        return jnp.transpose(jnp.concatenate(parts, axis=0)).astype(BF16)

    def own_sums(dx, sums):
        result = []
        for image in range(2):
            raw = dot(patches(image, dx, 128, 128), w1[...])
            result.append(sums[2 * image] + rows_sum(raw))
            result.append(sums[2 * image + 1] + rows_sum(raw * raw))
        return tuple(result)

    start = tuple(jnp.zeros((8, 384), F32) for _ in range(4))
    sums = lax.fori_loop(4, 12, own_sums, start)

    def per_channel(s):
        s = jnp.sum(s, axis=0, keepdims=True)
        return s[:, 64:128] + s[:, 128:192] + s[:, 192:256] + s[:, 256:320]

    def stat_tile(sum_f, sq_f, sum_m, sq_m):
        return jnp.concatenate(
            [
                jnp.concatenate([sum_f, sum_m], axis=1),
                jnp.concatenate([sq_f, sq_m], axis=1),
                jnp.zeros((6, 128), F32),
            ],
            axis=0,
        )

    tile = stat_tile(*[per_channel(s) for s in sums])

    def raw_fixed():
        def step(dx, carry):
            p = patches(0, dx, 0, 384)
            raw1f[dx - 3] = dot(p[96:288], w1[...])
            return carry

        lax.fori_loop(3, 13, step, 0)

    def raw_moving(d0, d1):
        def step(dx, carry):
            raw1m[dx] = dot(patches(1, dx, 0, 384), w1[...])
            return carry

        lax.fori_loop(d0, d1, step, 0)

    tile = total_over_devices(
        tile, peers, (ax1, ay1, az1), as1, ar1,
        (raw_fixed, lambda: raw_moving(0, 8), lambda: raw_moving(8, 16)),
    )

    def scale_and_offset(tile, gain, shift):
        mean = tile[0:1] / CELLS
        mean_sq = tile[1:2] / CELLS
        inv_dev = lax.rsqrt(mean_sq - mean * mean + 1e-05)
        scale = inv_dev * gain
        offset = shift - mean * scale
        pairs = []
        for image in range(2):
            half = slice(image * 64, image * 64 + 64)
            pairs.append(
                tuple(jnp.concatenate([a[:, half], a[:, half]], axis=1) for a in (scale, offset))
            )
        return pairs

    i_i, o_i = iota((64, 128), 0), iota((64, 128), 1) % 64
    perm = jnp.where(i_i == 2 * (o_i % 32) + o_i // 32, 1.0, 0.0)
    gains = jnp.concatenate([g1[...], s1[...], jnp.zeros((6, 64), F32)], axis=0)
    gains = jnp.dot(gains, perm, preferred_element_type=F32, precision=lax.Precision.HIGHEST)
    pairs = scale_and_offset(tile, gains[0:1], gains[1:2])

    def depth_inside(d):
        g = depth * 8 + d
        return jnp.where(jnp.logical_and(g >= 0, g < 32), 1.0, 0.0)

    def feat(raw, x, image, dx, out_dx, rows):
        keep = depth_inside(dx - 4)
        scale, offset = pairs[image][0] * keep, pairs[image][1] * keep
        for s in range(3):
            y = leaky(raw[out_dx, :, s * 128 : (s + 1) * 128] * scale + offset)
            x[s, out_dx] = (y * wmask[s, rows]).astype(BF16)

    def feat_fixed(dx, carry):
        feat(raw1f, xf, 0, dx, dx - 3, slice(96, 288))
        return carry

    def feat_moving(dx, carry):
        feat(raw1m, xm, 1, dx, dx, slice(0, 384))
        return carry

    lax.fori_loop(3, 13, feat_fixed, 0)
    lax.fori_loop(0, 16, feat_moving, 0)

    def second(x, od, spans):
        parts = []
        for a in range(3):
            for b in range(3):
                for s in range(3):
                    got = [x[s, od + a, (h + b) * 32 : (h + b + n) * 32, :] for h, n in spans]
                    parts.append(got[0] if len(got) == 1 else jnp.concatenate(got, axis=0))
        return dot(jnp.concatenate(parts, axis=1), wbig[...])

    def own_second(d, sums):
        raw_f = second(xf, d, ((0, 4),))
        raw2f[d] = raw_f
        raw_m = second(xm, d + 3, ((3, 4),))
        raw2m[d + 3, 96:224, :] = raw_m
        return (
            sums[0] + rows_sum(raw_f),
            sums[1] + rows_sum(raw_f * raw_f),
            sums[2] + rows_sum(raw_m),
            sums[3] + rows_sum(raw_m * raw_m),
        )

    start = tuple(jnp.zeros((8, 256), F32) for _ in range(4))
    sums = lax.fori_loop(0, 8, own_second, start)

    def per_channel_two(s):
        s = jnp.sum(s, axis=0, keepdims=True)
        return s[:, :64] + s[:, 64:128] + s[:, 128:192] + s[:, 192:]

    tile = stat_tile(*[per_channel_two(s) for s in sums])

    def planes(d0, d1):
        def step(od, carry):
            raw2m[od] = second(xm, od, ((0, 10),))
            return carry

        lax.fori_loop(d0, d1, step, 0)

    def sides():
        def step(od, carry):
            raw = second(xm, od, ((0, 3), (7, 3)))
            raw2m[od, 0:96, :] = raw[:96]
            raw2m[od, 224:320, :] = raw[96:]
            return carry

        lax.fori_loop(3, 11, step, 0)

    tile = total_over_devices(
        tile, peers, (ax2, ay2, az2), as2, ar2,
        (lambda: planes(0, 3), lambda: planes(11, 14), sides),
    )
    gain2 = jnp.concatenate([g2[...], g2[...]], axis=1)
    shift2 = jnp.concatenate([s2[...], s2[...]], axis=1)
    pairs2 = scale_and_offset(tile, gain2, shift2)

    def rounded(y):
        return leaky(y).astype(BF16).astype(F32)

    def spread_fixed(d, carry):
        scale, offset = pairs2[0]
        for h in range(4):
            for c in range(2):
                y = raw2f[d, h * 32 : (h + 1) * 32, c * 128 : (c + 1) * 128] * scale + offset
                ff[c, pl.ds(d * 4 + h, 32, stride=32), :] = rounded(y)
        return carry

    lax.fori_loop(0, 8, spread_fixed, 0)

    def spread_moving(od, carry):
        keep_d = depth_inside(od - 3)
        for oh in range(10):
            gh = height * 4 - 3 + oh
            keep = jnp.where(jnp.logical_and(gh >= 0, gh < 128), keep_d, 0.0)
            scale, offset = pairs2[1][0] * keep, pairs2[1][1] * keep
            for c in range(2):
                y = raw2m[od, oh * 32 : (oh + 1) * 32, c * 128 : (c + 1) * 128] * scale + offset
                kf[c, pl.ds(160 + oh * 16 + od, 32, stride=160), :] = rounded(y)
        return carry

    lax.fori_loop(0, 14, spread_moving, 0)

    k_i, n_i = iota((512, 128), 0), iota((512, 128), 1)
    hit = jnp.logical_and(
        n_i < 12, (k_i // 256) * 2 + (k_i % 128) // 64 == n_i // 3
    )
    ones = jnp.where(hit, 1.0, 0.0).astype(BF16)
    row, lane = iota((160, 128), 0), iota((160, 128), 1)
    dd, hh = row % 16 - (lane - 12), row // 16 - (lane - 20)
    bad_d = jnp.logical_and(
        jnp.logical_and(lane >= 12, lane < 20), jnp.logical_or(dd < 0, dd > 6)
    )
    bad_h = jnp.logical_and(
        jnp.logical_and(lane >= 20, lane < 24), jnp.logical_or(hh < 0, hh > 6)
    )
    base = jnp.where(jnp.logical_or(bad_d, bad_h), -BIG, 0.0)
    third = lane % 3

    def keys(q, carry):
        at = pl.ds(pl.multiple_of(q * 160, 160), 160)
        squares = []
        for c in range(2):
            m = kf[c, at, :]
            kb[c, at, :] = m.astype(BF16)
            sq = m * m
            hi = sq.astype(BF16)
            squares += [hi, (sq - hi.astype(F32)).astype(BF16)]
        norm = dot(jnp.concatenate(squares, axis=1), ones)
        hi = norm.astype(BF16).astype(F32)
        rest = norm - hi
        mid = rest.astype(BF16).astype(F32)
        term = jnp.where(third == 0, hi, jnp.where(third == 1, mid, rest - mid))
        e = jnp.where(lane == 24 + q % 4, 1.0, base)
        ke[at, :] = jnp.where(lane < 12, term, e).astype(BF16)
        return carry

    lax.fori_loop(0, 34, keys, 0)

    rate = sharp[0] * (math.log2(math.e) / 64.0)
    low = iota((64, 128), 1) < 64
    sub = iota((8, 256), 0).astype(F32)
    n_i = iota((1, 256), 1)
    q_w = (4 * ((n_i // 32) % 2) + n_i // 64).astype(F32)
    q_d = ((n_i // 4) % 8).astype(F32)
    q_h = (n_i % 4).astype(F32)
    tiles = [(phase, rel) for phase in range(4) for rel in range(4)
             if (phase, rel) not in ((0, 0), (3, 3))]

    def block(R, carry):
        at = pl.ds(pl.multiple_of(R * 64, 64), 64)
        a, b = 2.0 * ff[0, at, :], 2.0 * ff[1, at, :]
        ra, rb = pltpu.roll(a, 64, 1), pltpu.roll(b, 64, 1)
        first = jnp.concatenate([jnp.where(low, t, 0.0) for t in (a, ra, b, rb)], axis=0)
        second_ = jnp.concatenate([jnp.where(low, 0.0, t) for t in (ra, a, rb, b)], axis=0)
        query = (first.astype(BF16), second_.astype(BF16))
        odd = R % 2
        best = jnp.full((8, 256), -jnp.inf, F32)
        for phase in range(4):
            rels = [rel for p, rel in tiles if p == phase]
            count = len(rels) * 160
            rows = pl.ds(pl.multiple_of((2 * R + rels[0]) * 160, 160), count)
            lhs = jnp.concatenate([kb[phase // 2, rows, :], ke[rows, :]], axis=1)
            rhs = jnp.concatenate([query[phase % 2], qe[odd, phase]], axis=1)
            score = dot_nt(lhs, rhs)
            place = tiles.index((phase, rels[0])) * 160
            sbuf[place : place + count, :] = score
            best = jnp.maximum(best, jnp.max(score.reshape(count // 8, 8, 256), axis=0))
        top = jnp.broadcast_to(jnp.max(best, axis=0, keepdims=True), (8, 256))
        zero = jnp.zeros((8, 256), F32)
        by_h = [zero] * 10
        upper, total, w_sum = zero, zero, zero
        for n, (phase, rel) in enumerate(tiles):
            tile_sum = zero
            for oh in range(10):
                at_row = n * 160 + oh * 16
                p0 = jnp.exp2((sbuf[at_row : at_row + 8, :] - top) * rate)
                p1 = jnp.exp2((sbuf[at_row + 8 : at_row + 16, :] - top) * rate)
                both = p0 + p1
                upper = upper + p1
                by_h[oh] = by_h[oh] + both
                tile_sum = tile_sum + both
            total = total + tile_sum
            w_sum = w_sum + tile_sum * float(4 * (rel - 1) + phase)
        h_sum = zero
        for oh in range(1, 10):
            h_sum = h_sum + by_h[oh] * float(oh)
        d_sum = total * sub + 8.0 * upper
        weight = jnp.sum(total, axis=0, keepdims=True)

        def mean(s):
            return jnp.sum(s, axis=0, keepdims=True) / weight

        res[0, pl.ds(R, 1), :] = mean(d_sum) - (q_d + 3.0)
        res[1, pl.ds(R, 1), :] = mean(h_sum) - (q_h + 3.0)
        res[2, pl.ds(R, 1), :] = mean(w_sum) - q_w
        return carry

    lax.fori_loop(0, 16, block, 0)

    k_i, w_i = iota((128, 128), 0), iota((128, 128), 1)
    g, blk = k_i // 16, k_i % 16
    order = jnp.where(w_i == blk * 8 + (g % 2) * 4 + g // 2, 1.0, 0.0)
    for component in range(3):
        t = jnp.transpose(res[component])
        t = jnp.concatenate([t[n * 32 : (n + 1) * 32] for n in range(8)], axis=1)
        out[component] = jnp.dot(
            t, order, preferred_element_type=F32, precision=lax.Precision.HIGHEST
        )


def local(fi, mi, c1, g1, s1, c2, g2, s2, sharp):
    c1 = jnp.pad(c1.reshape(64, 27), ((0, 0), (0, 101)))
    vec = lambda a: a.reshape(1, 64)
    vmem = pl.BlockSpec(memory_space=pltpu.VMEM)
    tile = lambda n: pltpu.VMEM((n, 8, 128), F32)
    dma = lambda n: pltpu.SemaphoreType.DMA((n,))
    result = pl.pallas_call(
        kernel,
        out_shape=jax.ShapeDtypeStruct((3, 32, 128), F32),
        in_specs=[vmem] * 8 + [pl.BlockSpec(memory_space=pltpu.SMEM)],
        out_specs=vmem,
        scratch_shapes=[
            pltpu.VMEM((4, 2, 8, 128), F32),
            pltpu.VMEM((14, 2, 24, 128), F32),
            pltpu.VMEM((512, 1024), BF16),
            pltpu.VMEM((27 * 32, 128), F32),
            pltpu.VMEM((3456, 256), BF16),
            pltpu.VMEM((216, 384), BF16),
            pltpu.VMEM((4, 4, 192, 128), F32),
            pltpu.VMEM((3, 4, 192, 384), F32),
            pltpu.VMEM((10, 192, 384), F32),
            pltpu.VMEM((16, 384, 384), F32),
            pltpu.VMEM((3, 384, 128), F32),
            pltpu.VMEM((3, 10, 192, 128), BF16),
            pltpu.VMEM((3, 16, 384, 128), BF16),
            pltpu.VMEM((8, 128, 256), F32),
            pltpu.VMEM((14, 320, 256), F32),
            pltpu.VMEM((2, 1024, 128), F32),
            pltpu.VMEM((2, 34 * 160, 128), F32),
            pltpu.VMEM((2, 34 * 160, 128), BF16),
            pltpu.VMEM((34 * 160, 128), BF16),
            pltpu.VMEM((2, 4, 256, 128), BF16),
            pltpu.VMEM((14 * 160, 256), F32),
            pltpu.VMEM((3, 16, 256), F32),
            tile(8), tile(4), tile(4), tile(8), tile(4), tile(4),
            dma(14), dma(14), dma(13), dma(13), dma(13), dma(13),
        ],
        compiler_params=pltpu.CompilerParams(
            collective_id=0, has_side_effects=True, vmem_limit_bytes=60 * 1024 * 1024
        ),
    )(fi, mi, c1, vec(g1), vec(s1), c2, vec(g2), vec(s2), sharp)
    return result.reshape(3, 8, 4, 128)


def solution(mesh):
    placed = (P("depth", "height", None),) * 2 + (P(),) * 7
    return jax.shard_map(
        local,
        mesh=mesh,
        in_specs=placed,
        out_specs=P(None, "depth", "height", None),
        check_vma=False,
    )
```

```python
import math

import jax
import jax.numpy as jnp
from jax import lax
from jax.experimental import pallas as pl
from jax.experimental.pallas import tpu as pltpu
from jax.sharding import PartitionSpec as P

MESH = pl.DeviceIdType.MESH
F32, BF16, I32 = jnp.float32, jnp.bfloat16, jnp.int32
BIG = 1e30
CELLS = 32 * 128 * 128
HALO = [(dd, hh) for hh in (-2, -1, 0, 1, 2) for dd in (-1, 0, 1) if (dd, hh) != (0, 0)]
HEIGHT_SPAN = {0: (0, 4, 5), 1: (0, 4, 1), 2: (3, 4, 0), -1: (0, 4, 9), -2: (0, 1, 13)}


def iota(shape, dim):
    return lax.broadcasted_iota(I32, shape, dim)


def dot(a, b):
    return jnp.dot(a, b, preferred_element_type=F32)


def dot_nt(a, b):
    return lax.dot_general(a, b, (((1,), (1,)), ((), ())), preferred_element_type=F32)


def rows_sum(x):
    return jnp.sum(x.reshape(x.shape[0] // 8, 8, x.shape[1]), axis=0)


def position():
    depth, height = lax.axis_index("depth"), lax.axis_index("height")
    return depth, height


def group_peers(depth, height):
    x_hi, zy = height // 16, height % 16
    plane = [(depth, x_hi * 16 + (zy + k) % 16) for k in range(1, 16)]
    along_x = []
    for k in range(1, 8):
        g = (x_hi * 4 + depth + k) % 8
        along_x.append((g % 4, (g // 4) * 16 + zy))
    return plane, along_x


def halo_peers(depth, height):
    return [((depth + dd + 4) % 4, (height + hh + 32) % 32) for dd, hh in HALO]


def total_over_devices(value, peers, bufs, send_sems, recv_sems, works):
    count = 0
    for group, buf, work in zip(peers, bufs, works):
        buf[0] = value
        copies = []
        for k, peer in enumerate(group):
            copy = pltpu.make_async_remote_copy(
                src_ref=buf.at[0],
                dst_ref=buf.at[k + 1],
                send_sem=send_sems.at[count],
                recv_sem=recv_sems.at[count],
                device_id=peer,
                device_id_type=MESH,
            )
            copy.start()
            copies.append(copy)
            count += 1
        work()
        for copy in copies:
            copy.wait()
        value = jnp.sum(buf[...], axis=0)
    return value


def leaky(v):
    return jnp.maximum(v, 0.01 * v)


def kernel(
    fi_h, mi_h, c1_h, g1_h, s1_h, c2_h, g2_h, s2_h, sharp,
    out,
    fi, mi, c1, g1, s1, c2, g2, s2,
    own, ext, selm, wf, wbig, w1, v, vs, raw1f, raw1m, wmask, xf, xm,
    raw2f, raw2m, ff, kf, kb, ke, qe, sbuf, sbuf2, res,
    ap1, ax1, ap2, ax2,
    hs, hr, as1, ar1, as2, ar2, ins,
):
    depth, height = position()
    halo = halo_peers(depth, height)
    peers = group_peers(depth, height)

    barrier = pltpu.get_barrier_semaphore()
    everyone = halo + peers[0] + peers[1]
    for peer in everyone:
        pl.semaphore_signal(barrier, inc=1, device_id=peer, device_id_type=MESH)
    pairs_in = [(fi_h, fi), (mi_h, mi), (c2_h, c2), (c1_h, c1), (g1_h, g1), (s1_h, s1), (g2_h, g2), (s2_h, s2)]
    loads = [pltpu.make_async_copy(a, b, ins.at[n]) for n, (a, b) in enumerate(pairs_in)]
    for load in loads:
        load.start()
    loads[0].wait()
    loads[1].wait()
    for h in range(4):
        own[h, 0] = fi[:, h, :]
        own[h, 1] = mi[:, h, :]
    pl.semaphore_wait(barrier, len(everyone))

    copies = []
    for n, (dd, hh) in enumerate(HALO):
        h0, h1, land = HEIGHT_SPAN[hh]
        block = 8 - 8 * dd
        copy = pltpu.make_async_remote_copy(
            src_ref=own.at[pl.ds(h0, h1 - h0)],
            dst_ref=ext.at[pl.ds(land, h1 - h0), :, pl.ds(block, 8), :],
            send_sem=hs.at[n],
            recv_sem=hr.at[n],
            device_id=halo[n],
            device_id_type=MESH,
        )
        copy.start()
        copies.append(copy)

    for load in loads[2:]:
        load.wait()
    ext[5:9, :, 8:16, :] = own[...]
    n_i = iota((1, 1024), 1)
    want = 4 * (n_i & 31) - 2 + (n_i >> 7)
    near = jnp.where(iota((128, 1024), 0) == want, 1.0, 0.0)
    for hh in range(4):
        part = jnp.where(((n_i >> 5) & 3) == hh, near, 0.0)
        selm[hh * 128 : (hh + 1) * 128, :] = part.astype(BF16)
    for pair in range(32):
        wf[pl.ds(pair, 27, stride=32), :] = c2[:, pair * 128 : (pair + 1) * 128].astype(F32)

    def build(ab, carry):
        zero = jnp.zeros((64, 64), F32)
        taps = []
        for c in range(3):
            t = wf[pl.ds(pl.multiple_of((ab * 3 + c) * 32, 32), 32), :]
            taps.append(jnp.concatenate([t[:, :64], t[:, 64:]], axis=0))
        for u in range(6):
            parts = [taps[u - wo] if 0 <= u - wo <= 2 else zero for wo in range(4)]
            row = jnp.concatenate(parts, axis=1).astype(BF16)
            wbig[pl.ds(pl.multiple_of((ab * 6 + u) * 64, 64), 64), :] = row
        return carry

    lax.fori_loop(0, 9, build, 0)

    r_i, k_i = iota((64, 64), 0), iota((64, 64), 1)
    even_first = jnp.where(r_i == 2 * (k_i & 31) + (k_i >> 5), 1.0, 0.0)
    c1t = jnp.concatenate([c1[...].reshape(27, 64), jnp.zeros((5, 64), F32)], axis=0)
    c1t = jnp.dot(c1t, even_first, preferred_element_type=F32, precision=lax.Precision.HIGHEST)
    zero = jnp.zeros((32, 64), F32)
    spread = jnp.concatenate(
        [jnp.concatenate([c1t if q == u else zero for q in range(6)], axis=1) for u in range(6)],
        axis=0,
    )
    spread_hi = spread.astype(BF16)
    spread_lo = (spread - spread_hi.astype(F32)).astype(BF16)
    r_i, k_i = iota((72, 192), 0), iota((72, 192), 1)
    tap = k_i % 32
    hit = jnp.logical_and(
        tap // 3 == ((r_i // 8) % 3) * 3 + r_i // 24,
        jnp.logical_and(r_i % 8 - k_i // 32 == tap % 3, tap < 27),
    )
    pick = jnp.where(hit, 1.0, 0.0).astype(BF16)
    w1_hi, w1_lo = dot(pick, spread_hi), dot(pick, spread_lo)
    w1[...] = jnp.concatenate([w1_hi, w1_hi, w1_lo], axis=0).astype(BF16)

    row, lane = iota((384, 128), 0), iota((384, 128), 1)
    gh = height * 4 - 4 + row // 32
    inside = jnp.logical_and(gh >= 0, gh < 128)
    wmask[0] = jnp.where(
        jnp.logical_and(inside, jnp.logical_or(row % 32 > 0, lane >= 64)), 1.0, 0.0
    )
    wmask[1] = jnp.where(inside, 1.0, 0.0)
    wmask[2] = jnp.where(
        jnp.logical_and(inside, jnp.logical_or(row % 32 < 31, lane < 64)), 1.0, 0.0
    )
    q_i, lane = iota((256, 128), 0), iota((256, 128), 1)
    w_q = q_i >> 5
    e_q = jnp.where(lane - 12 == ((q_i >> 2) & 7), 1.0, 0.0)
    e_q = jnp.where(jnp.logical_and(lane >= 20, lane - 20 == (q_i & 3)), 1.0, e_q)
    lane1 = iota((1, 128), 1)
    in_quad = jnp.logical_and(lane1 >= 24, lane1 < 28)
    for odd in range(2):
        for phase in range(4):
            norm_lane = jnp.logical_and(lane1 < 8, (lane1 >> 1) == phase)
            w_k = 4 * (((lane1 - 24 - 2 * odd + 8) & 3) - 1) + phase
            w_k = jnp.where(in_quad, w_k, w_q)
            e = jnp.where(jnp.abs(w_k - w_q) > 3, -BIG, e_q)
            qe[odd, phase] = jnp.where(norm_lane, -1.0, e).astype(BF16)
    kf[...] = jnp.zeros_like(kf)

    for copy in copies:
        copy.wait()

    row = iota((48, 128), 0)
    gd = depth * 8 - 8 + row % 24
    d_in = jnp.logical_and(gd >= 0, gd < 32)
    stacks = []
    for h4 in range(4):
        parts = []
        for hh in range(4):
            hx = h4 * 4 + hh
            if hx >= 14:
                parts.append(jnp.zeros((96, 128), BF16))
                continue
            x = ext[hx].reshape(48, 128)
            gh = jnp.full((48, 128), height * 4 - 5 + hx, I32)
            ok = jnp.logical_and(d_in, jnp.logical_and(gh >= 0, gh < 128))
            x = jnp.where(ok, x, 0.0)
            hi = x.astype(BF16)
            lo = (x - hi.astype(F32)).astype(BF16)
            parts.append(jnp.concatenate([hi, lo], axis=0))
        stacks.append(jnp.concatenate(parts, axis=1))
    for h4 in range(4):
        picked = dot(stacks[h4], selm[...])
        for q in range(4):
            for j in range(8):
                v[q, h4, pl.ds(j, 24, stride=8), :] = picked[
                    q * 24 : q * 24 + 24, j * 128 : (j + 1) * 128
                ]
    for q in range(4):
        full = jnp.concatenate([v[q, h4] for h4 in range(4)], axis=1)
        for b in range(3):
            vs[b, q] = full[:, 32 * b : 32 * b + 384]

    def patches(image, dx, lane0, lanes):
        start = pl.multiple_of((dx + 3) * 8, 8)
        parts = [
            vs[b, hl * 2 + image, pl.ds(start, 24), lane0 : lane0 + lanes]
            for hl in (0, 1, 0)
            for b in range(3)
        ]
        return jnp.transpose(jnp.concatenate(parts, axis=0)).astype(BF16)

    def own_sums(dx, sums):
        result = []
        for image in range(2):
            raw = dot(patches(image, dx, 128, 128), w1[...])
            result.append(sums[2 * image] + rows_sum(raw))
            result.append(sums[2 * image + 1] + rows_sum(raw * raw))
        return tuple(result)

    start = tuple(jnp.zeros((8, 384), F32) for _ in range(4))
    sums = lax.fori_loop(4, 12, own_sums, start)

    def per_channel(s):
        s = jnp.sum(s, axis=0, keepdims=True)
        return s[:, 64:128] + s[:, 128:192] + s[:, 192:256] + s[:, 256:320]

    def stat_tile(sum_f, sq_f, sum_m, sq_m):
        return jnp.concatenate(
            [
                jnp.concatenate([sum_f, sum_m], axis=1),
                jnp.concatenate([sq_f, sq_m], axis=1),
            ],
            axis=0,
        )

    tile = stat_tile(*[per_channel(s) for s in sums])

    def raw_fixed():
        def step(dx, carry):
            p = patches(0, dx, 0, 384)
            raw1f[dx - 3] = dot(p[96:288], w1[...])
            return carry

        lax.fori_loop(3, 13, step, 0)

    def raw_moving(d0, d1):
        def step(dx, carry):
            raw1m[dx] = dot(patches(1, dx, 0, 384), w1[...])
            return carry

        lax.fori_loop(d0, d1, step, 0)

    def raw_first():
        raw_fixed()
        raw_moving(0, 8)

    tile = total_over_devices(
        tile, peers, (ap1, ax1), as1, ar1, (raw_first, lambda: raw_moving(8, 16)),
    )

    def scale_and_offset(tile, gain, shift):
        mean = tile[0:1] / CELLS
        mean_sq = tile[1:2] / CELLS
        inv_dev = lax.rsqrt(mean_sq - mean * mean + 1e-05)
        scale = inv_dev * gain
        offset = shift - mean * scale
        pairs = []
        for image in range(2):
            half = slice(image * 64, image * 64 + 64)
            pairs.append(
                tuple(jnp.concatenate([a[:, half], a[:, half]], axis=1) for a in (scale, offset))
            )
        return pairs

    i_i, o_i = iota((64, 128), 0), iota((64, 128), 1) % 64
    perm = jnp.where(i_i == 2 * (o_i % 32) + o_i // 32, 1.0, 0.0)
    gains = jnp.concatenate([g1[...], s1[...], jnp.zeros((6, 64), F32)], axis=0)
    gains = jnp.dot(gains, perm, preferred_element_type=F32, precision=lax.Precision.HIGHEST)
    pairs = scale_and_offset(tile, gains[0:1], gains[1:2])

    def depth_inside(d):
        g = depth * 8 + d
        return jnp.where(jnp.logical_and(g >= 0, g < 32), 1.0, 0.0)

    def feat(raw, x, image, dx, out_dx, rows):
        keep = depth_inside(dx - 4)
        scale, offset = pairs[image][0] * keep, pairs[image][1] * keep
        for s in range(3):
            y = leaky(raw[out_dx, :, s * 128 : (s + 1) * 128] * scale + offset)
            x[s, out_dx] = (y * wmask[s, rows]).astype(BF16)

    def feat_fixed(dx, carry):
        feat(raw1f, xf, 0, dx, dx - 3, slice(96, 288))
        return carry

    def feat_moving(dx, carry):
        feat(raw1m, xm, 1, dx, dx, slice(0, 384))
        return carry

    lax.fori_loop(3, 13, feat_fixed, 0)
    lax.fori_loop(0, 16, feat_moving, 0)

    def second(x, od, spans):
        parts = []
        for a in range(3):
            for b in range(3):
                for s in range(3):
                    got = [x[s, od + a, (h + b) * 32 : (h + b + n) * 32, :] for h, n in spans]
                    parts.append(got[0] if len(got) == 1 else jnp.concatenate(got, axis=0))
        return dot(jnp.concatenate(parts, axis=1), wbig[...])

    def own_second(d, sums):
        raw_f = second(xf, d, ((0, 4),))
        raw2f[d] = raw_f
        raw_m = second(xm, d + 3, ((3, 4),))
        raw2m[d + 3, 96:224, :] = raw_m
        return (
            sums[0] + rows_sum(raw_f),
            sums[1] + rows_sum(raw_f * raw_f),
            sums[2] + rows_sum(raw_m),
            sums[3] + rows_sum(raw_m * raw_m),
        )

    start = tuple(jnp.zeros((8, 256), F32) for _ in range(4))
    sums = lax.fori_loop(0, 8, own_second, start)

    def per_channel_two(s):
        s = jnp.sum(s, axis=0, keepdims=True)
        return s[:, :64] + s[:, 64:128] + s[:, 128:192] + s[:, 192:]

    tile = stat_tile(*[per_channel_two(s) for s in sums])

    def planes(d0, d1):
        def step(od, carry):
            raw2m[od] = second(xm, od, ((0, 10),))
            return carry

        lax.fori_loop(d0, d1, step, 0)

    def sides():
        def step(od, carry):
            raw = second(xm, od, ((0, 3), (7, 3)))
            raw2m[od, 0:96, :] = raw[:96]
            raw2m[od, 224:320, :] = raw[96:]
            return carry

        lax.fori_loop(3, 11, step, 0)

    def both_ends():
        planes(0, 3)
        planes(11, 14)

    tile = total_over_devices(
        tile, peers, (ap2, ax2), as2, ar2, (both_ends, sides),
    )
    gain2 = jnp.concatenate([g2[...], g2[...]], axis=1)
    shift2 = jnp.concatenate([s2[...], s2[...]], axis=1)
    pairs2 = scale_and_offset(tile, gain2, shift2)

    def rounded(y):
        return leaky(y).astype(BF16).astype(F32)

    def spread_fixed(d, carry):
        scale, offset = pairs2[0]
        for h in range(4):
            for c in range(2):
                y = raw2f[d, h * 32 : (h + 1) * 32, c * 128 : (c + 1) * 128] * scale + offset
                ff[c, pl.ds(d * 4 + h, 32, stride=32), :] = rounded(y)
        return carry

    lax.fori_loop(0, 8, spread_fixed, 0)

    def spread_moving(od, carry):
        keep_d = depth_inside(od - 3)
        for oh in range(10):
            gh = height * 4 - 3 + oh
            keep = jnp.where(jnp.logical_and(gh >= 0, gh < 128), keep_d, 0.0)
            scale, offset = pairs2[1][0] * keep, pairs2[1][1] * keep
            for c in range(2):
                y = raw2m[od, oh * 32 : (oh + 1) * 32, c * 128 : (c + 1) * 128] * scale + offset
                kf[c, pl.ds(160 + oh * 16 + od, 32, stride=160), :] = leaky(y)
        return carry

    lax.fori_loop(0, 14, spread_moving, 0)

    k_i, n_i = iota((512, 128), 0), iota((512, 128), 1)
    hit = jnp.logical_and(n_i < 8, (k_i >> 8) * 2 + ((k_i >> 6) & 1) == (n_i >> 1))
    ones = jnp.where(hit, 1.0, 0.0).astype(BF16)
    row, lane = iota((160, 128), 0), iota((160, 128), 1)
    dd, hh = (row & 15) - (lane - 12), (row >> 4) - (lane - 20)
    bad_d = jnp.logical_and(
        jnp.logical_and(lane >= 12, lane < 20), jnp.logical_or(dd < 0, dd > 6)
    )
    bad_h = jnp.logical_and(
        jnp.logical_and(lane >= 20, lane < 24), jnp.logical_or(hh < 0, hh > 6)
    )
    base = jnp.where(jnp.logical_or(bad_d, bad_h), -BIG, 0.0)
    base = jnp.concatenate([base, base], axis=0)
    lane = iota((320, 128), 1)
    mark = lane - (iota((320, 128), 0) >= 160).astype(I32)
    odd_lane = (iota((1, 128), 1) & 1) == 1

    def keys(q, carry):
        at = pl.ds(pl.multiple_of(q * 320, 320), 320)
        squares = []
        for c in range(2):
            m = kf[c, at, :].astype(BF16)
            kb[c, at, :] = m
            m = m.astype(F32)
            sq = m * m
            hi = sq.astype(BF16)
            squares += [hi, (sq - hi.astype(F32)).astype(BF16)]
        norm = dot(jnp.concatenate(squares, axis=1), ones)
        hi = norm.astype(BF16).astype(F32)
        term = norm - jnp.where(odd_lane, hi, 0.0)
        e = jnp.where(mark == 24 + 2 * (q & 1), 1.0, base)
        ke[at, :] = (term + e).astype(BF16)
        return carry

    lax.fori_loop(0, 17, keys, 0)

    rate = sharp[0] * (math.log2(math.e) / 64.0)
    low = iota((32, 128), 1) < 64
    sub = iota((8, 128), 0).astype(F32)
    n_i = iota((1, 128), 1)
    q_w = (n_i >> 5).astype(F32)
    q_d = ((n_i >> 2) & 7).astype(F32)
    q_h = (n_i & 3).astype(F32)
    tiles = [
        [(p, r) for p in range(4) for r in range(4) if -3 <= 4 * (r - 1) + p - 4 * quad <= 6]
        for quad in range(2)
    ]
    zero = jnp.zeros((8, 128), F32)

    def queries(R):
        first, other = [], []
        for quad in range(2):
            at = pl.ds(pl.multiple_of(R * 64 + quad * 32, 32), 32)
            a, b = 2.0 * ff[0, at, :], 2.0 * ff[1, at, :]
            ra, rb = pltpu.roll(a, 64, 1), pltpu.roll(b, 64, 1)
            first += [jnp.where(low, t, 0.0) for t in (a, ra, b, rb)]
            other += [jnp.where(low, 0.0, t) for t in (ra, a, rb, b)]
        return [jnp.concatenate(t, axis=0).astype(BF16) for t in (first, other)]

    def scores(R, query, phase, buf, best):
        rels = [rel for rel in range(4) if any((phase, rel) in t for t in tiles)]
        count = len(rels) * 160
        rows = pl.ds(pl.multiple_of((2 * R + rels[0]) * 160, 160), count)
        lhs = jnp.concatenate([kb[phase // 2, rows, :], ke[rows, :]], axis=1)
        rhs = jnp.concatenate([query[phase % 2], qe[R & 1, phase]], axis=1)
        score = dot_nt(lhs, rhs)
        for n, rel in enumerate(rels):
            for quad in range(2):
                if (phase, rel) not in tiles[quad]:
                    continue
                place = (quad * 10 + tiles[quad].index((phase, rel))) * 160
                part = score[n * 160 : n * 160 + 160, quad * 128 : quad * 128 + 128]
                buf[place : place + 160, :] = part
                best[quad] = jnp.maximum(best[quad], jnp.max(part.reshape(20, 8, 128), axis=0))

    def weigh(quad, which, buf, top, state):
        for n in which:
            phase, rel = tiles[quad][n]
            tile_sum = zero
            for oh in range(10):
                at_row = (quad * 10 + n) * 160 + oh * 16
                p0 = jnp.exp2(buf[at_row : at_row + 8, :] * rate - top)
                p1 = jnp.exp2(buf[at_row + 8 : at_row + 16, :] * rate - top)
                both = p0 + p1
                state["upper"] = state["upper"] + p1
                state[oh] = state[oh] + both
                tile_sum = tile_sum + both
            state["total"] = state["total"] + tile_sum
            state["w"] = state["w"] + tile_sum * float(4 * (rel - 1) + phase - 4 * quad)

    def finish(R, quad, state):
        h_sum = zero
        for oh in range(1, 10):
            h_sum = h_sum + state[oh] * float(oh)
        d_sum = state["total"] * sub + 8.0 * state["upper"]
        weight = jnp.sum(state["total"], axis=0, keepdims=True)
        for n, (s, own_at) in enumerate(
            ((d_sum, q_d + 3.0), (h_sum, q_h + 3.0), (state["w"], q_w))
        ):
            mean = jnp.sum(s, axis=0, keepdims=True) / weight
            res[n * 2 + quad, pl.ds(R, 1), :] = mean - own_at

    def step(R, buf, best, R_next, buf_next):
        query = queries(R_next)
        best_next = [jnp.full((8, 128), -jnp.inf, F32) for _ in range(2)]
        for quad in range(2):
            top = jnp.max(best[quad], axis=0, keepdims=True) * rate
            top = jnp.broadcast_to(top, (8, 128))
            state = {k: zero for k in list(range(10)) + ["upper", "total", "w"]}
            for half in range(2):
                scores(R_next, query, quad * 2 + half, buf_next, best_next)
                weigh(quad, range(half * 5, half * 5 + 5), buf, top, state)
            finish(R, quad, state)
        return best_next

    def two_blocks(i, best):
        best = step(2 * i, sbuf, list(best), 2 * i + 1, sbuf2)
        best = step(2 * i + 1, sbuf2, best, jnp.minimum(2 * i + 2, 15), sbuf)
        return tuple(best)

    best = [jnp.full((8, 128), -jnp.inf, F32) for _ in range(2)]
    query = queries(0)
    for phase in range(4):
        scores(0, query, phase, sbuf, best)
    lax.fori_loop(0, 8, two_blocks, tuple(best))

    k_i, w_i = iota((128, 128), 0), iota((128, 128), 1)
    order = jnp.where(w_i == (k_i & 15) * 8 + (k_i >> 4), 1.0, 0.0)
    for component in range(3):
        t = [jnp.transpose(res[component * 2 + quad]) for quad in range(2)]
        t = [t[n // 4][(n % 4) * 32 : (n % 4) * 32 + 32] for n in range(8)]
        t = jnp.concatenate(t, axis=1)
        out[component] = jnp.dot(
            t, order, preferred_element_type=F32, precision=lax.Precision.HIGHEST
        )


def local(fi, mi, c1, g1, s1, c2, g2, s2, sharp):
    c1 = jnp.transpose(c1, (2, 3, 4, 1, 0)).reshape(27, 1, 64)
    vec = lambda a: a.reshape(1, 64)
    vmem = pl.BlockSpec(memory_space=pltpu.VMEM)
    tile = lambda n: pltpu.VMEM((n, 2, 128), F32)
    dma = lambda n: pltpu.SemaphoreType.DMA((n,))
    result = pl.pallas_call(
        kernel,
        out_shape=jax.ShapeDtypeStruct((3, 32, 128), F32),
        in_specs=[pl.BlockSpec(memory_space=pl.ANY)] * 8 + [pl.BlockSpec(memory_space=pltpu.SMEM)],
        out_specs=vmem,
        scratch_shapes=[
            pltpu.VMEM((8, 4, 128), F32),
            pltpu.VMEM((8, 4, 128), F32),
            pltpu.VMEM((27, 1, 64), F32),
            pltpu.VMEM((1, 64), F32),
            pltpu.VMEM((1, 64), F32),
            pltpu.VMEM((27, 4096), BF16),
            pltpu.VMEM((1, 64), F32),
            pltpu.VMEM((1, 64), F32),
            pltpu.VMEM((4, 2, 8, 128), F32),
            pltpu.VMEM((14, 2, 24, 128), F32),
            pltpu.VMEM((512, 1024), BF16),
            pltpu.VMEM((27 * 32, 128), F32),
            pltpu.VMEM((3456, 256), BF16),
            pltpu.VMEM((216, 384), BF16),
            pltpu.VMEM((4, 4, 192, 128), F32),
            pltpu.VMEM((3, 4, 192, 384), F32),
            pltpu.VMEM((10, 192, 384), F32),
            pltpu.VMEM((16, 384, 384), F32),
            pltpu.VMEM((3, 384, 128), F32),
            pltpu.VMEM((3, 10, 192, 128), BF16),
            pltpu.VMEM((3, 16, 384, 128), BF16),
            pltpu.VMEM((8, 128, 256), F32),
            pltpu.VMEM((14, 320, 256), F32),
            pltpu.VMEM((2, 1024, 128), F32),
            pltpu.VMEM((2, 34 * 160, 128), F32),
            pltpu.VMEM((2, 34 * 160, 128), BF16),
            pltpu.VMEM((34 * 160, 128), BF16),
            pltpu.VMEM((2, 4, 256, 128), BF16),
            pltpu.VMEM((20 * 160, 128), F32),
            pltpu.VMEM((20 * 160, 128), F32),
            pltpu.VMEM((6, 16, 128), F32),
            tile(16), tile(8), tile(16), tile(8),
            dma(14), dma(14), dma(22), dma(22), dma(22), dma(22), dma(8),
        ],
        compiler_params=pltpu.CompilerParams(
            collective_id=0, has_side_effects=True, vmem_limit_bytes=60 * 1024 * 1024
        ),
    )(fi, mi, c1, vec(g1), vec(s1), c2, vec(g2), vec(s2), sharp)
    return result.reshape(3, 8, 4, 128)


def solution(mesh):
    placed = (P("depth", "height", None),) * 2 + (P(),) * 7
    return jax.shard_map(
        local,
        mesh=mesh,
        in_specs=placed,
        out_specs=P(None, "depth", "height", None),
        check_vma=False,
    )
```

```python
import math

import jax
import jax.numpy as jnp
from jax import lax
from jax.experimental import pallas as pl
from jax.experimental.pallas import tpu as pltpu
from jax.sharding import PartitionSpec as P

MESH = pl.DeviceIdType.MESH
F32, BF16, I32 = jnp.float32, jnp.bfloat16, jnp.int32
BIG = 1e30
CELLS = 32 * 128 * 128
HALO = [(dd, hh) for hh in (-2, -1, 0, 1, 2) for dd in (-1, 0, 1) if (dd, hh) != (0, 0)]
HEIGHT_SPAN = {0: (0, 4, 5), 1: (0, 4, 1), 2: (3, 4, 0), -1: (0, 4, 9), -2: (0, 1, 13)}


def iota(shape, dim):
    return lax.broadcasted_iota(I32, shape, dim)


def dot(a, b):
    return jnp.dot(a, b, preferred_element_type=F32)


def dot_nt(a, b):
    return lax.dot_general(a, b, (((1,), (1,)), ((), ())), preferred_element_type=F32)


def rows_sum(x):
    return jnp.sum(x.reshape(x.shape[0] // 8, 8, x.shape[1]), axis=0)


def position():
    depth, height = lax.axis_index("depth"), lax.axis_index("height")
    return depth, height


def group_peers(depth, height):
    x_hi, zy = height // 16, height % 16
    plane = [(depth, x_hi * 16 + (zy + k) % 16) for k in range(1, 16)]
    along_x = []
    for k in range(1, 8):
        g = (x_hi * 4 + depth + k) % 8
        along_x.append((g % 4, (g // 4) * 16 + zy))
    return plane, along_x


def halo_peers(depth, height):
    return [((depth + dd + 4) % 4, (height + hh + 32) % 32) for dd, hh in HALO]


def total_over_devices(value, peers, bufs, send_sems, recv_sems, works):
    count = 0
    for group, buf, work in zip(peers, bufs, works):
        buf[0] = value
        copies = []
        for k, peer in enumerate(group):
            copy = pltpu.make_async_remote_copy(
                src_ref=buf.at[0],
                dst_ref=buf.at[k + 1],
                send_sem=send_sems.at[count],
                recv_sem=recv_sems.at[count],
                device_id=peer,
                device_id_type=MESH,
            )
            copy.start()
            copies.append(copy)
            count += 1
        work()
        for copy in copies:
            copy.wait()
        value = jnp.sum(buf[...], axis=0)
    return value


def leaky(v):
    return jnp.maximum(v, 0.01 * v)


def kernel(
    fi_h, mi_h, c1_h, g1_h, s1_h, c2_h, g2_h, s2_h, sharp,
    out,
    fi, mi, c1, g1, s1, c2, g2, s2,
    own, ext, selm, wf, wbig, w1, v, vs, raw1f, raw1m, xf, xm,
    ff, kf, kb, ke, qe, sbuf, sbuf2, res,
    ap1, ax1, ap2, ax2,
    hs, hr, as1, ar1, as2, ar2, ins,
):
    depth, height = position()
    halo = halo_peers(depth, height)
    peers = group_peers(depth, height)

    barrier = pltpu.get_barrier_semaphore()
    everyone = halo + peers[0] + peers[1]
    for peer in everyone:
        pl.semaphore_signal(barrier, inc=1, device_id=peer, device_id_type=MESH)
    pairs_in = [(fi_h, fi), (mi_h, mi), (c2_h, c2), (c1_h, c1), (g1_h, g1), (s1_h, s1), (g2_h, g2), (s2_h, s2)]
    loads = [pltpu.make_async_copy(a, b, ins.at[n]) for n, (a, b) in enumerate(pairs_in)]
    for load in loads:
        load.start()
    loads[0].wait()
    loads[1].wait()
    for h in range(4):
        own[h, 0] = fi[:, h, :]
        own[h, 1] = mi[:, h, :]
    pl.semaphore_wait(barrier, len(everyone))

    copies = []
    for n, (dd, hh) in enumerate(HALO):
        h0, h1, land = HEIGHT_SPAN[hh]
        block = 8 - 8 * dd
        copy = pltpu.make_async_remote_copy(
            src_ref=own.at[pl.ds(h0, h1 - h0)],
            dst_ref=ext.at[pl.ds(land, h1 - h0), :, pl.ds(block, 8), :],
            send_sem=hs.at[n],
            recv_sem=hr.at[n],
            device_id=halo[n],
            device_id_type=MESH,
        )
        copy.start()
        copies.append(copy)

    for load in loads[2:]:
        load.wait()
    ext[5:9, :, 8:16, :] = own[...]
    n_i = iota((1, 1024), 1)
    want = 4 * (n_i & 31) - 2 + (n_i >> 7)
    near = jnp.where(iota((128, 1024), 0) == want, 1.0, 0.0)
    for hh in range(4):
        part = jnp.where(((n_i >> 5) & 3) == hh, near, 0.0)
        selm[hh * 128 : (hh + 1) * 128, :] = part.astype(BF16)
    for pair in range(32):
        wf[pl.ds(pair, 27, stride=32), :] = c2[:, pair * 128 : (pair + 1) * 128].astype(F32)

    def build(ab, carry):
        zero = jnp.zeros((64, 64), F32)
        taps = []
        for c in range(3):
            t = wf[pl.ds(pl.multiple_of((ab * 3 + c) * 32, 32), 32), :]
            taps.append(jnp.concatenate([t[:, :64], t[:, 64:]], axis=0))
        for u in range(6):
            parts = [taps[u - wo] if 0 <= u - wo <= 2 else zero for wo in range(4)]
            row = jnp.concatenate(parts, axis=1).astype(BF16)
            wbig[pl.ds(pl.multiple_of((ab * 6 + u) * 64, 64), 64), :] = row
        return carry

    lax.fori_loop(0, 9, build, 0)

    r_i, k_i = iota((64, 64), 0), iota((64, 64), 1)
    even_first = jnp.where(r_i == 2 * (k_i & 31) + (k_i >> 5), 1.0, 0.0)
    c1t = jnp.concatenate([c1[...].reshape(27, 64), jnp.zeros((5, 64), F32)], axis=0)
    c1t = jnp.dot(c1t, even_first, preferred_element_type=F32, precision=lax.Precision.HIGHEST)
    zero = jnp.zeros((32, 64), F32)
    spread = jnp.concatenate(
        [jnp.concatenate([c1t if q == u else zero for q in range(6)], axis=1) for u in range(6)],
        axis=0,
    )
    spread_hi = spread.astype(BF16)
    spread_lo = (spread - spread_hi.astype(F32)).astype(BF16)
    r_i, k_i = iota((72, 192), 0), iota((72, 192), 1)
    tap = k_i % 32
    hit = jnp.logical_and(
        tap // 3 == ((r_i // 8) % 3) * 3 + r_i // 24,
        jnp.logical_and(r_i % 8 - k_i // 32 == tap % 3, tap < 27),
    )
    pick = jnp.where(hit, 1.0, 0.0).astype(BF16)
    w1_hi, w1_lo = dot(pick, spread_hi), dot(pick, spread_lo)
    w1[...] = jnp.concatenate([w1_hi, w1_hi, w1_lo], axis=0).astype(BF16)

    q_i, lane = iota((256, 128), 0), iota((256, 128), 1)
    w_q = q_i >> 5
    e_q = jnp.where(lane - 12 == ((q_i >> 2) & 7), 1.0, 0.0)
    e_q = jnp.where(jnp.logical_and(lane >= 20, lane - 20 == (q_i & 3)), 1.0, e_q)
    lane1 = iota((1, 128), 1)
    in_quad = jnp.logical_and(lane1 >= 24, lane1 < 28)
    for odd in range(2):
        for phase in range(4):
            norm_lane = jnp.logical_and(lane1 < 8, (lane1 >> 1) == phase)
            w_k = 4 * (((lane1 - 24 - 2 * odd + 8) & 3) - 1) + phase
            w_k = jnp.where(in_quad, w_k, w_q)
            e = jnp.where(jnp.abs(w_k - w_q) > 3, -BIG, e_q)
            qe[odd, phase] = jnp.where(norm_lane, -1.0, e).astype(BF16)
    kf[...] = jnp.zeros_like(kf)

    for copy in copies:
        copy.wait()

    row = iota((48, 128), 0)
    gd = depth * 8 - 8 + row % 24
    d_in = jnp.logical_and(gd >= 0, gd < 32)

    def pick_rows(h4):
        parts = []
        for hh in range(4):
            hx = h4 * 4 + hh
            if hx >= 14:
                parts.append(jnp.zeros((96, 128), BF16))
                continue
            x = ext[hx].reshape(48, 128)
            gh = jnp.full((48, 128), height * 4 - 5 + hx, I32)
            ok = jnp.logical_and(d_in, jnp.logical_and(gh >= 0, gh < 128))
            x = jnp.where(ok, x, 0.0)
            hi = x.astype(BF16)
            lo = (x - hi.astype(F32)).astype(BF16)
            parts.append(jnp.concatenate([hi, lo], axis=0))
        picked = dot(jnp.concatenate(parts, axis=1), selm[...])
        for q in range(4):
            for j in range(8):
                v[q, h4, pl.ds(j, 24, stride=8), :] = picked[
                    q * 24 : q * 24 + 24, j * 128 : (j + 1) * 128
                ]

    def shifted(column, rows):
        for q in range(4):
            full = jnp.concatenate([v[q, column, rows], v[q, column + 1, rows]], axis=1)
            for b in range(3):
                vs[b, q, rows, column * 128 : column * 128 + 128] = full[:, 32 * b : 32 * b + 128]

    own_rows = slice(56, 136)
    pick_rows(1)
    pick_rows(2)
    shifted(1, own_rows)

    def patches(image, dx, lane0, lanes):
        start = pl.multiple_of((dx + 3) * 8, 8)
        parts = [
            vs[b, hl * 2 + image, pl.ds(start, 24), lane0 : lane0 + lanes]
            for hl in (0, 1, 0)
            for b in range(3)
        ]
        return jnp.transpose(jnp.concatenate(parts, axis=0)).astype(BF16)

    def own_sums(dx, sums):
        result = []
        for image in range(2):
            lhs = [patches(image, 2 * dx + n, 128, 128) for n in range(2)]
            raw = dot(jnp.concatenate(lhs, axis=0), w1[...])
            result.append(sums[2 * image] + rows_sum(raw))
            result.append(sums[2 * image + 1] + rows_sum(raw * raw))
        return tuple(result)

    start = tuple(jnp.zeros((8, 384), F32) for _ in range(4))
    sums = lax.fori_loop(2, 6, own_sums, start)

    def per_channel(s):
        s = jnp.sum(s, axis=0, keepdims=True)
        return s[:, 64:128] + s[:, 128:192] + s[:, 192:256] + s[:, 256:320]

    def stat_tile(sum_f, sq_f, sum_m, sq_m):
        return jnp.concatenate(
            [
                jnp.concatenate([sum_f, sum_m], axis=1),
                jnp.concatenate([sq_f, sq_m], axis=1),
            ],
            axis=0,
        )

    tile = stat_tile(*[per_channel(s) for s in sums])

    def raw_fixed():
        def step(dx, carry):
            p = patches(0, dx, 0, 384)
            raw1f[dx - 3] = dot(p[96:288], w1[...])
            return carry

        lax.fori_loop(3, 13, step, 0)

    def raw_moving(d0, d1):
        def step(dx, carry):
            raw1m[dx] = dot(patches(1, dx, 0, 384), w1[...])
            return carry

        lax.fori_loop(d0, d1, step, 0)

    def raw_first():
        pick_rows(0)
        pick_rows(3)
        shifted(1, slice(0, 56))
        shifted(1, slice(136, 192))
        shifted(0, slice(0, 192))
        shifted(2, slice(0, 192))
        raw_fixed()
        raw_moving(0, 8)

    tile = total_over_devices(
        tile, peers, (ap1, ax1), as1, ar1, (raw_first, lambda: raw_moving(8, 16)),
    )

    def scale_and_offset(tile, gain, shift):
        mean = tile[0:1] / CELLS
        mean_sq = tile[1:2] / CELLS
        inv_dev = lax.rsqrt(mean_sq - mean * mean + 1e-05)
        scale = inv_dev * gain
        offset = shift - mean * scale
        pairs = []
        for image in range(2):
            half = slice(image * 64, image * 64 + 64)
            pairs.append(
                tuple(jnp.concatenate([a[:, half], a[:, half]], axis=1) for a in (scale, offset))
            )
        return pairs

    i_i, o_i = iota((64, 128), 0), iota((64, 128), 1) % 64
    perm = jnp.where(i_i == 2 * (o_i % 32) + o_i // 32, 1.0, 0.0)
    gains = jnp.concatenate([g1[...], s1[...], jnp.zeros((6, 64), F32)], axis=0)
    gains = jnp.dot(gains, perm, preferred_element_type=F32, precision=lax.Precision.HIGHEST)
    pairs = scale_and_offset(tile, gains[0:1], gains[1:2])

    def depth_inside(d):
        g = depth * 8 + d
        return jnp.where(jnp.logical_and(g >= 0, g < 32), 1.0, 0.0)

    def height_inside(h):
        g = height * 4 + h
        return jnp.where(jnp.logical_and(g >= 0, g < 128), 1.0, 0.0)

    row, lane = iota((8, 128), 0), iota((8, 128), 1)
    not_before = jnp.logical_or(row > 0, lane >= 64)
    not_after = jnp.logical_or(row < 7, lane < 64)

    def feat(raw, x, image, d, raw_d, x_d, rows, hxs):
        keep_d = depth_inside(d)
        for n, hx in enumerate(hxs):
            keep = keep_d * height_inside(hx - 4)
            scale, offset = pairs[image][0] * keep, pairs[image][1] * keep
            at = slice(rows + n * 32, rows + n * 32 + 32)
            for s in range(3):
                y = leaky(raw[raw_d, at, s * 128 : (s + 1) * 128] * scale + offset)
                if s == 0:
                    y = jnp.concatenate([jnp.where(not_before, y[:8], 0.0), y[8:]], axis=0)
                if s == 2:
                    y = jnp.concatenate([y[:24], jnp.where(not_after, y[24:], 0.0)], axis=0)
                x[s, x_d, at, :] = y.astype(BF16)

    def feat_near(dx, carry):
        feat(raw1f, xf, 0, dx - 4, dx - 3, dx - 3, 0, range(3, 9))
        feat(raw1m, xm, 1, dx - 4, dx, dx, 96, range(3, 9))
        return carry

    lax.fori_loop(3, 13, feat_near, 0)

    def feat_plane(dx, carry):
        feat(raw1m, xm, 1, dx - 4, dx, dx, 0, range(12))
        return carry

    def feat_sides(dx, carry):
        feat(raw1m, xm, 1, dx - 4, dx, dx, 0, range(3))
        feat(raw1m, xm, 1, dx - 4, dx, dx, 288, range(9, 12))
        return carry

    def second(x, od, spans):
        parts = []
        for a in range(3):
            for b in range(3):
                for s in range(3):
                    got = [x[s, od + a, (h + b) * 32 : (h + b + n) * 32, :] for h, n in spans]
                    parts.append(got[0] if len(got) == 1 else jnp.concatenate(got, axis=0))
        return dot(jnp.concatenate(parts, axis=1), wbig[...])

    def put_keys(raw, od, rows):
        for n, oh in enumerate(rows):
            for c in range(2):
                part = raw[n * 32 : (n + 1) * 32, c * 128 : (c + 1) * 128]
                kf[c, pl.ds(164 + oh * 16 + od, 32, stride=164), :] = part

    def own_second(d, sums):
        raw_f = second(xf, d, ((0, 4),))
        for h in range(4):
            for c in range(2):
                part = raw_f[h * 32 : (h + 1) * 32, c * 128 : (c + 1) * 128]
                ff[c, pl.ds(d * 4 + h, 32, stride=36), :] = part
        raw_m = second(xm, d + 3, ((3, 4),))
        put_keys(raw_m, d + 3, range(3, 7))
        return (
            sums[0] + rows_sum(raw_f),
            sums[1] + rows_sum(raw_f * raw_f),
            sums[2] + rows_sum(raw_m),
            sums[3] + rows_sum(raw_m * raw_m),
        )

    start = tuple(jnp.zeros((8, 256), F32) for _ in range(4))
    sums = lax.fori_loop(0, 8, own_second, start)

    def per_channel_two(s):
        s = jnp.sum(s, axis=0, keepdims=True)
        return s[:, :64] + s[:, 64:128] + s[:, 128:192] + s[:, 192:]

    tile = stat_tile(*[per_channel_two(s) for s in sums])

    def planes(d0, d1):
        def step(od, carry):
            put_keys(second(xm, od, ((0, 10),)), od, range(10))
            return carry

        lax.fori_loop(d0, d1, step, 0)

    def sides():
        def step(od, carry):
            raw = second(xm, od, ((0, 3), (7, 3)))
            put_keys(raw, od, (0, 1, 2, 7, 8, 9))
            return carry

        lax.fori_loop(3, 11, step, 0)

    def both_ends():
        lax.fori_loop(0, 3, feat_plane, 0)
        lax.fori_loop(13, 16, feat_plane, 0)
        lax.fori_loop(3, 13, feat_sides, 0)
        planes(0, 3)
        planes(11, 14)

    tile = total_over_devices(
        tile, peers, (ap2, ax2), as2, ar2, (both_ends, sides),
    )
    gain2 = jnp.concatenate([g2[...], g2[...]], axis=1)
    shift2 = jnp.concatenate([s2[...], s2[...]], axis=1)
    pairs2 = scale_and_offset(tile, gain2, shift2)

    def rounded(y):
        return leaky(y).astype(BF16).astype(F32)

    k_i, n_i = iota((512, 128), 0), iota((512, 128), 1)
    hit = jnp.logical_and(n_i < 8, (k_i >> 8) * 2 + ((k_i >> 6) & 1) == (n_i >> 1))
    ones = jnp.where(hit, 1.0, 0.0).astype(BF16)
    row, lane = iota((160, 128), 0), iota((160, 128), 1)
    dd, hh = (row & 15) - (lane - 12), (row >> 4) - (lane - 20)
    bad_d = jnp.logical_and(
        jnp.logical_and(lane >= 12, lane < 20), jnp.logical_or(dd < 0, dd > 6)
    )
    bad_h = jnp.logical_and(
        jnp.logical_and(lane >= 20, lane < 24), jnp.logical_or(hh < 0, hh > 6)
    )
    base = jnp.where(jnp.logical_or(bad_d, bad_h), -BIG, 0.0)
    base = jnp.concatenate([base, base], axis=0)
    lane = iota((320, 128), 1)
    mark = lane - (iota((320, 128), 0) >= 160).astype(I32)
    row = iota((320, 128), 0)
    row = jnp.where(row >= 160, row - 160, row)
    gd, gh = depth * 8 - 3 + (row & 15), height * 4 - 3 + (row >> 4)
    keep = jnp.logical_and(
        jnp.logical_and(gd >= 0, gd < 32), jnp.logical_and(gh >= 0, gh < 128)
    )
    keep = jnp.where(jnp.logical_and(keep, (row & 15) < 14), 1.0, 0.0)
    scale_m, offset_m = pairs2[1]
    odd_lane = (iota((1, 128), 1) & 1) == 1

    def keys(q, carry):
        at = pl.ds(pl.multiple_of(q * 320, 320), 320)
        squares = []
        for c in range(2):
            m = jnp.concatenate([kf[c, pl.ds(q * 328 + n * 164, 160), :] for n in range(2)], axis=0)
            m = (leaky(m * scale_m + offset_m) * keep).astype(BF16)
            kb[c, at, :] = m
            m = m.astype(F32)
            sq = m * m
            hi = sq.astype(BF16)
            squares += [hi, (sq - hi.astype(F32)).astype(BF16)]
        norm = dot(jnp.concatenate(squares, axis=1), ones)
        hi = norm.astype(BF16).astype(F32)
        term = norm - jnp.where(odd_lane, hi, 0.0)
        e = jnp.where(mark == 24 + 2 * (q & 1), 1.0, base)
        ke[at, :] = (term + e).astype(BF16)
        return carry

    lax.fori_loop(0, 17, keys, 0)
    for q in (0, 33):
        at = slice(q * 160, q * 160 + 160)
        kb[:, at, :] = jnp.zeros((2, 160, 128), BF16)
        ke[at, :] = jnp.where(lane[:160] == 24 + q % 4, 1.0, base[:160]).astype(BF16)

    rate = sharp[0] * (math.log2(math.e) / 64.0)
    low = iota((32, 128), 1) < 64
    sub = iota((8, 128), 0).astype(F32)
    n_i = iota((1, 128), 1)
    q_w = (n_i >> 5).astype(F32)
    q_d = ((n_i >> 2) & 7).astype(F32)
    q_h = (n_i & 3).astype(F32)
    tiles = [
        [(p, r) for p in range(4) for r in range(4) if -3 <= 4 * (r - 1) + p - 4 * quad <= 6]
        for quad in range(2)
    ]
    zero = jnp.zeros((8, 128), F32)

    def queries(R):
        first, other = [], []
        for quad in range(2):
            at = pl.ds(R * 72 + quad * 36, 32)
            a, b = (
                2.0 * rounded(ff[c, at, :] * pairs2[0][0] + pairs2[0][1]) for c in range(2)
            )
            ra, rb = pltpu.roll(a, 64, 1), pltpu.roll(b, 64, 1)
            first += [jnp.where(low, t, 0.0) for t in (a, ra, b, rb)]
            other += [jnp.where(low, 0.0, t) for t in (ra, a, rb, b)]
        return [jnp.concatenate(t, axis=0).astype(BF16) for t in (first, other)]

    def scores(R, query, phase, buf, best):
        rels = [rel for rel in range(4) if any((phase, rel) in t for t in tiles)]
        count = len(rels) * 160
        rows = pl.ds(pl.multiple_of((2 * R + rels[0]) * 160, 160), count)
        lhs = jnp.concatenate([kb[phase // 2, rows, :], ke[rows, :]], axis=1)
        rhs = jnp.concatenate([query[phase % 2], qe[R & 1, phase]], axis=1)
        score = dot_nt(lhs, rhs)
        for n, rel in enumerate(rels):
            for quad in range(2):
                if (phase, rel) not in tiles[quad]:
                    continue
                place = (quad * 10 + tiles[quad].index((phase, rel))) * 160
                part = score[n * 160 : n * 160 + 160, quad * 128 : quad * 128 + 128]
                buf[place : place + 160, :] = part
                best[quad] = jnp.maximum(best[quad], jnp.max(part.reshape(20, 8, 128), axis=0))

    def weigh(quad, which, buf, top, state):
        for n in which:
            phase, rel = tiles[quad][n]
            tile_sum = zero
            for oh in range(10):
                at_row = (quad * 10 + n) * 160 + oh * 16
                p0 = jnp.exp2(buf[at_row : at_row + 8, :] * rate - top)
                p1 = jnp.exp2(buf[at_row + 8 : at_row + 16, :] * rate - top)
                both = p0 + p1
                state["upper"] = state["upper"] + p1
                state[oh] = state[oh] + both
                tile_sum = tile_sum + both
            state["total"] = state["total"] + tile_sum
            state["w"] = state["w"] + tile_sum * float(4 * (rel - 1) + phase - 4 * quad)

    def finish(R, quad, state):
        h_sum = zero
        for oh in range(1, 10):
            h_sum = h_sum + state[oh] * float(oh)
        d_sum = state["total"] * sub + 8.0 * state["upper"]
        weight = jnp.sum(state["total"], axis=0, keepdims=True)
        for n, (s, own_at) in enumerate(
            ((d_sum, q_d + 3.0), (h_sum, q_h + 3.0), (state["w"], q_w))
        ):
            mean = jnp.sum(s, axis=0, keepdims=True) / weight
            res[n * 2 + quad, pl.ds(R, 1), :] = mean - own_at

    def step(R, buf, best, R_next, buf_next):
        query = queries(R_next)
        best_next = [jnp.full((8, 128), -jnp.inf, F32) for _ in range(2)]
        for quad in range(2):
            top = jnp.max(best[quad], axis=0, keepdims=True) * rate
            top = jnp.broadcast_to(top, (8, 128))
            state = {k: zero for k in list(range(10)) + ["upper", "total", "w"]}
            for half in range(2):
                scores(R_next, query, quad * 2 + half, buf_next, best_next)
                weigh(quad, range(half * 5, half * 5 + 5), buf, top, state)
            finish(R, quad, state)
        return best_next

    def two_blocks(i, best):
        best = step(2 * i, sbuf, list(best), 2 * i + 1, sbuf2)
        best = step(2 * i + 1, sbuf2, best, jnp.minimum(2 * i + 2, 15), sbuf)
        return tuple(best)

    best = [jnp.full((8, 128), -jnp.inf, F32) for _ in range(2)]
    query = queries(0)
    for phase in range(4):
        scores(0, query, phase, sbuf, best)
    lax.fori_loop(0, 8, two_blocks, tuple(best))

    k_i, w_i = iota((128, 128), 0), iota((128, 128), 1)
    order = jnp.where(w_i == (k_i & 15) * 8 + (k_i >> 4), 1.0, 0.0)
    for component in range(3):
        t = [jnp.transpose(res[component * 2 + quad]) for quad in range(2)]
        t = [t[n // 4][(n % 4) * 32 : (n % 4) * 32 + 32] for n in range(8)]
        t = jnp.concatenate(t, axis=1)
        out[component] = jnp.dot(
            t, order, preferred_element_type=F32, precision=lax.Precision.HIGHEST
        )


def local(fi, mi, c1, g1, s1, c2, g2, s2, sharp):
    c1 = jnp.transpose(c1, (2, 3, 4, 1, 0)).reshape(27, 1, 64)
    vec = lambda a: a.reshape(1, 64)
    vmem = pl.BlockSpec(memory_space=pltpu.VMEM)
    tile = lambda n: pltpu.VMEM((n, 2, 128), F32)
    dma = lambda n: pltpu.SemaphoreType.DMA((n,))
    result = pl.pallas_call(
        kernel,
        out_shape=jax.ShapeDtypeStruct((3, 32, 128), F32),
        in_specs=[pl.BlockSpec(memory_space=pl.ANY)] * 8 + [pl.BlockSpec(memory_space=pltpu.SMEM)],
        out_specs=vmem,
        scratch_shapes=[
            pltpu.VMEM((8, 4, 128), F32),
            pltpu.VMEM((8, 4, 128), F32),
            pltpu.VMEM((27, 1, 64), F32),
            pltpu.VMEM((1, 64), F32),
            pltpu.VMEM((1, 64), F32),
            pltpu.VMEM((27, 4096), BF16),
            pltpu.VMEM((1, 64), F32),
            pltpu.VMEM((1, 64), F32),
            pltpu.VMEM((4, 2, 8, 128), F32),
            pltpu.VMEM((14, 2, 24, 128), F32),
            pltpu.VMEM((512, 1024), BF16),
            pltpu.VMEM((27 * 32, 128), F32),
            pltpu.VMEM((3456, 256), BF16),
            pltpu.VMEM((216, 384), BF16),
            pltpu.VMEM((4, 4, 192, 128), F32),
            pltpu.VMEM((3, 4, 192, 384), F32),
            pltpu.VMEM((10, 192, 384), F32),
            pltpu.VMEM((16, 384, 384), F32),
            pltpu.VMEM((3, 10, 192, 128), BF16),
            pltpu.VMEM((3, 16, 384, 128), BF16),
            pltpu.VMEM((2, 32 * 36, 128), F32),
            pltpu.VMEM((2, 34 * 164, 128), F32),
            pltpu.VMEM((2, 34 * 160, 128), BF16),
            pltpu.VMEM((34 * 160, 128), BF16),
            pltpu.VMEM((2, 4, 256, 128), BF16),
            pltpu.VMEM((20 * 160, 128), F32),
            pltpu.VMEM((20 * 160, 128), F32),
            pltpu.VMEM((6, 16, 128), F32),
            tile(16), tile(8), tile(16), tile(8),
            dma(14), dma(14), dma(22), dma(22), dma(22), dma(22), dma(8),
        ],
        compiler_params=pltpu.CompilerParams(
            collective_id=0, has_side_effects=True, vmem_limit_bytes=60 * 1024 * 1024
        ),
    )(fi, mi, c1, vec(g1), vec(s1), c2, vec(g2), vec(s2), sharp)
    return result.reshape(3, 8, 4, 128)


def solution(mesh):
    placed = (P("depth", "height", None),) * 2 + (P(),) * 7
    return jax.shard_map(
        local,
        mesh=mesh,
        in_specs=placed,
        out_specs=P(None, "depth", "height", None),
        check_vma=False,
    )
```

```python
import math

import jax
import jax.numpy as jnp
from jax import lax
from jax.experimental import pallas as pl
from jax.experimental.pallas import tpu as pltpu
from jax.sharding import PartitionSpec as P

MESH = pl.DeviceIdType.MESH
F32, BF16, I32 = jnp.float32, jnp.bfloat16, jnp.int32
BIG = 1e30
CELLS = 32 * 128 * 128
HALO = [(dd, hh) for hh in (-2, -1, 0, 1, 2) for dd in (-1, 0, 1) if (dd, hh) != (0, 0)]
HEIGHT_SPAN = {0: (0, 4, 5), 1: (0, 4, 1), 2: (3, 4, 0), -1: (0, 4, 9), -2: (0, 1, 13)}


def iota(shape, dim):
    return lax.broadcasted_iota(I32, shape, dim)


def dot(a, b):
    return jnp.dot(a, b, preferred_element_type=F32)


def dot_nt(a, b):
    return lax.dot_general(a, b, (((1,), (1,)), ((), ())), preferred_element_type=F32)


def rows_sum(x):
    return jnp.sum(x.reshape(x.shape[0] // 8, 8, x.shape[1]), axis=0)


def position():
    depth, height = lax.axis_index("depth"), lax.axis_index("height")
    return depth, height


def group_peers(depth, height):
    x_hi, zy = height // 16, height % 16
    plane = [(depth, x_hi * 16 + (zy + k) % 16) for k in range(1, 16)]
    along_x = []
    for k in range(1, 8):
        g = (x_hi * 4 + depth + k) % 8
        along_x.append((g % 4, (g // 4) * 16 + zy))
    return plane, along_x


def halo_peers(depth, height):
    return [((depth + dd + 4) % 4, (height + hh + 32) % 32) for dd, hh in HALO]


def total_over_devices(value, peers, bufs, send_sems, recv_sems, works):
    for g, (group, buf, work) in enumerate(zip(peers, bufs, works)):
        buf[0] = value
        for k, peer in enumerate(group):
            pltpu.make_async_remote_copy(
                src_ref=buf.at[0],
                dst_ref=buf.at[k + 1],
                send_sem=send_sems.at[g],
                recv_sem=recv_sems.at[g],
                device_id=peer,
                device_id_type=MESH,
            ).start()
        work()
        tiles = buf.at[pl.ds(1, len(group))]
        pltpu.make_async_copy(tiles, tiles, recv_sems.at[g]).wait()
        pltpu.make_async_copy(tiles, tiles, send_sems.at[g]).wait()
        value = jnp.sum(buf[...], axis=0)
    return value


def leaky(v):
    return jnp.maximum(v, 0.01 * v)


def kernel(
    fi_h, mi_h, c1_h, g1_h, s1_h, c2_h, g2_h, s2_h, sharp,
    out,
    fi, mi, c1, g1, s1, c2, g2, s2,
    own, ext, selm, wf, wbig, w1, v, vs, raw1f, raw1m, xf, xm,
    ff, kf, kb, ke, qe, sbuf, sbuf2, res,
    ap1, ax1, ap2, ax2,
    hs, hr, as1, ar1, as2, ar2, ins,
):
    depth, height = position()
    halo = halo_peers(depth, height)
    peers = group_peers(depth, height)

    pairs_in = [(fi_h, fi), (mi_h, mi), (c2_h, c2), (c1_h, c1), (g1_h, g1), (s1_h, s1), (g2_h, g2), (s2_h, s2)]
    loads = [pltpu.make_async_copy(a, b, ins.at[n]) for n, (a, b) in enumerate(pairs_in)]
    for load in loads:
        load.start()
    barrier = pltpu.get_barrier_semaphore()
    everyone = halo + peers[0] + peers[1]
    for peer in everyone:
        pl.semaphore_signal(barrier, inc=1, device_id=peer, device_id_type=MESH)
    loads[0].wait()
    loads[1].wait()
    for h in range(4):
        own[h, 0] = fi[:, h, :]
        own[h, 1] = mi[:, h, :]
    pl.semaphore_wait(barrier, len(everyone))

    copies = []
    for n, (dd, hh) in enumerate(HALO):
        h0, h1, land = HEIGHT_SPAN[hh]
        block = 8 - 8 * dd
        which = {1: 0, -1: 1}.get(dd, 2 + (hh + 2 if hh < 0 else hh + 1))
        copy = pltpu.make_async_remote_copy(
            src_ref=own.at[pl.ds(h0, h1 - h0)],
            dst_ref=ext.at[pl.ds(land, h1 - h0), :, pl.ds(block, 8), :],
            send_sem=hs.at[which],
            recv_sem=hr.at[which],
            device_id=halo[n],
            device_id_type=MESH,
        )
        copy.start()
        if dd == 0:
            copies.append(copy)

    for load in loads[2:]:
        load.wait()
    ext[5:9, :, 8:16, :] = own[...]
    n_i = iota((1, 1024), 1)
    want = 4 * (n_i & 31) - 2 + (n_i >> 7)
    near = jnp.where(iota((128, 1024), 0) == want, 1.0, 0.0)
    for hh in range(4):
        part = jnp.where(((n_i >> 5) & 3) == hh, near, 0.0)
        selm[hh * 128 : (hh + 1) * 128, :] = part.astype(BF16)
    for pair in range(32):
        wf[pl.ds(pair, 27, stride=32), :] = c2[:, pair * 128 : (pair + 1) * 128].astype(F32)

    def build(ab, carry):
        zero = jnp.zeros((64, 64), F32)
        taps = []
        for c in range(3):
            t = wf[pl.ds(pl.multiple_of((ab * 3 + c) * 32, 32), 32), :]
            taps.append(jnp.concatenate([t[:, :64], t[:, 64:]], axis=0))
        for u in range(6):
            parts = [taps[u - wo] if 0 <= u - wo <= 2 else zero for wo in range(4)]
            row = jnp.concatenate(parts, axis=1).astype(BF16)
            wbig[pl.ds(pl.multiple_of((ab * 6 + u) * 64, 64), 64), :] = row
        return carry

    lax.fori_loop(0, 9, build, 0)

    r_i, k_i = iota((64, 64), 0), iota((64, 64), 1)
    even_first = jnp.where(r_i == 2 * (k_i & 31) + (k_i >> 5), 1.0, 0.0)
    c1t = jnp.concatenate([c1[...].reshape(27, 64), jnp.zeros((5, 64), F32)], axis=0)
    c1t = jnp.dot(c1t, even_first, preferred_element_type=F32, precision=lax.Precision.HIGHEST)
    zero = jnp.zeros((32, 64), F32)
    spread = jnp.concatenate(
        [jnp.concatenate([c1t if q == u else zero for q in range(6)], axis=1) for u in range(6)],
        axis=0,
    )
    spread_hi = spread.astype(BF16)
    spread_lo = (spread - spread_hi.astype(F32)).astype(BF16)
    r_i, k_i = iota((72, 192), 0), iota((72, 192), 1)
    tap = k_i % 32
    hit = jnp.logical_and(
        tap // 3 == ((r_i // 8) % 3) * 3 + r_i // 24,
        jnp.logical_and(r_i % 8 - k_i // 32 == tap % 3, tap < 27),
    )
    pick = jnp.where(hit, 1.0, 0.0).astype(BF16)
    w1_hi, w1_lo = dot(pick, spread_hi), dot(pick, spread_lo)
    w1[...] = jnp.concatenate([w1_hi, w1_hi, w1_lo], axis=0).astype(BF16)

    q_i, lane = iota((256, 128), 0), iota((256, 128), 1)
    w_q = q_i >> 5
    e_q = jnp.where(lane - 12 == ((q_i >> 2) & 7), 1.0, 0.0)
    e_q = jnp.where(jnp.logical_and(lane >= 20, lane - 20 == (q_i & 3)), 1.0, e_q)
    lane1 = iota((1, 128), 1)
    in_quad = jnp.logical_and(lane1 >= 24, lane1 < 28)
    for odd in range(2):
        for phase in range(4):
            norm_lane = jnp.logical_and(lane1 < 8, (lane1 >> 1) == phase)
            w_k = 4 * (((lane1 - 24 - 2 * odd + 8) & 3) - 1) + phase
            w_k = jnp.where(in_quad, w_k, w_q)
            e = jnp.where(jnp.abs(w_k - w_q) > 3, -BIG, e_q)
            qe[odd, phase] = jnp.where(norm_lane, -1.0, e).astype(BF16)
    kf[...] = jnp.zeros_like(kf)

    for copy in copies:
        copy.wait()
    for which, block in ((0, 0), (1, 16)):
        planes_in = ext.at[:, :, pl.ds(block, 8), :]
        pltpu.make_async_copy(planes_in, planes_in, hr.at[which]).wait()
        pltpu.make_async_copy(planes_in, planes_in, hs.at[which]).wait()

    row = iota((48, 128), 0)
    gd = depth * 8 - 8 + row % 24
    d_in = jnp.logical_and(gd >= 0, gd < 32)

    def pick_rows(h4):
        parts = []
        for hh in range(4):
            hx = h4 * 4 + hh
            if hx >= 14:
                parts.append(jnp.zeros((96, 128), BF16))
                continue
            x = ext[hx].reshape(48, 128)
            gh = jnp.full((48, 128), height * 4 - 5 + hx, I32)
            ok = jnp.logical_and(d_in, jnp.logical_and(gh >= 0, gh < 128))
            x = jnp.where(ok, x, 0.0)
            hi = x.astype(BF16)
            lo = (x - hi.astype(F32)).astype(BF16)
            parts.append(jnp.concatenate([hi, lo], axis=0))
        picked = dot(jnp.concatenate(parts, axis=1), selm[...])
        for q in range(4):
            for j in range(8):
                v[q, h4, pl.ds(j, 24, stride=8), :] = picked[
                    q * 24 : q * 24 + 24, j * 128 : (j + 1) * 128
                ]

    def shifted(column, rows):
        for q in range(4):
            full = jnp.concatenate([v[q, column, rows], v[q, column + 1, rows]], axis=1)
            for b in range(3):
                vs[b, q, rows, column * 128 : column * 128 + 128] = full[:, 32 * b : 32 * b + 128]

    own_rows = slice(56, 136)
    pick_rows(1)
    pick_rows(2)
    shifted(1, own_rows)

    def patches(image, dx, lane0, lanes):
        start = pl.multiple_of((dx + 3) * 8, 8)
        parts = [
            vs[b, hl * 2 + image, pl.ds(start, 24), lane0 : lane0 + lanes]
            for hl in (0, 1, 0)
            for b in range(3)
        ]
        return jnp.transpose(jnp.concatenate(parts, axis=0)).astype(BF16)

    def own_sums(dx, sums):
        result = []
        for image in range(2):
            lhs = [patches(image, 2 * dx + n, 128, 128) for n in range(2)]
            raw = dot(jnp.concatenate(lhs, axis=0), w1[...])
            result.append(sums[2 * image] + rows_sum(raw))
            result.append(sums[2 * image + 1] + rows_sum(raw * raw))
        return tuple(result)

    start = tuple(jnp.zeros((8, 384), F32) for _ in range(4))
    sums = lax.fori_loop(2, 6, own_sums, start)

    def per_channel(s):
        s = jnp.sum(s, axis=0, keepdims=True)
        return s[:, 64:128] + s[:, 128:192] + s[:, 192:256] + s[:, 256:320]

    def stat_tile(sum_f, sq_f, sum_m, sq_m):
        return jnp.concatenate(
            [
                jnp.concatenate([sum_f, sum_m], axis=1),
                jnp.concatenate([sq_f, sq_m], axis=1),
            ],
            axis=0,
        )

    tile = stat_tile(*[per_channel(s) for s in sums])

    def raw_fixed():
        def step(dx, carry):
            p = patches(0, dx, 0, 384)
            raw1f[dx - 3] = dot(p[96:288], w1[...])
            return carry

        lax.fori_loop(3, 13, step, 0)

    def raw_moving(d0, d1):
        def step(dx, carry):
            raw1m[dx] = dot(patches(1, dx, 0, 384), w1[...])
            return carry

        lax.fori_loop(d0, d1, step, 0)

    def raw_first():
        pick_rows(0)
        pick_rows(3)
        shifted(1, slice(0, 56))
        shifted(1, slice(136, 192))
        shifted(0, slice(0, 192))
        shifted(2, slice(0, 192))
        raw_fixed()
        raw_moving(0, 8)

    tile = total_over_devices(
        tile, peers, (ap1, ax1), as1, ar1, (raw_first, lambda: raw_moving(8, 16)),
    )

    def scale_and_offset(tile, gain, shift):
        mean = tile[0:1] / CELLS
        mean_sq = tile[1:2] / CELLS
        inv_dev = lax.rsqrt(mean_sq - mean * mean + 1e-05)
        scale = inv_dev * gain
        offset = shift - mean * scale
        pairs = []
        for image in range(2):
            half = slice(image * 64, image * 64 + 64)
            pairs.append(
                tuple(jnp.concatenate([a[:, half], a[:, half]], axis=1) for a in (scale, offset))
            )
        return pairs

    i_i, o_i = iota((64, 128), 0), iota((64, 128), 1) % 64
    perm = jnp.where(i_i == 2 * (o_i % 32) + o_i // 32, 1.0, 0.0)
    gains = jnp.concatenate([g1[...], s1[...], jnp.zeros((6, 64), F32)], axis=0)
    gains = jnp.dot(gains, perm, preferred_element_type=F32, precision=lax.Precision.HIGHEST)
    pairs = scale_and_offset(tile, gains[0:1], gains[1:2])

    def depth_inside(d):
        g = depth * 8 + d
        return jnp.where(jnp.logical_and(g >= 0, g < 32), 1.0, 0.0)

    def height_inside(h):
        g = height * 4 + h
        return jnp.where(jnp.logical_and(g >= 0, g < 128), 1.0, 0.0)

    row, lane = iota((8, 128), 0), iota((8, 128), 1)
    not_before = jnp.logical_or(row > 0, lane >= 64)
    not_after = jnp.logical_or(row < 7, lane < 64)

    def feat(raw, x, image, d, raw_d, x_d, rows, hxs):
        keep_d = depth_inside(d)
        for n, hx in enumerate(hxs):
            keep = keep_d * height_inside(hx - 4)
            scale, offset = pairs[image][0] * keep, pairs[image][1] * keep
            at = slice(rows + n * 32, rows + n * 32 + 32)
            for s in range(3):
                y = leaky(raw[raw_d, at, s * 128 : (s + 1) * 128] * scale + offset)
                if s == 0:
                    y = jnp.concatenate([jnp.where(not_before, y[:8], 0.0), y[8:]], axis=0)
                if s == 2:
                    y = jnp.concatenate([y[:24], jnp.where(not_after, y[24:], 0.0)], axis=0)
                x[s, x_d, at, :] = y.astype(BF16)

    def feat_near(dx, carry):
        feat(raw1f, xf, 0, dx - 4, dx - 3, dx - 3, 0, range(3, 9))
        feat(raw1m, xm, 1, dx - 4, dx, dx, 96, range(3, 9))
        return carry

    lax.fori_loop(3, 13, feat_near, 0)

    def feat_plane(dx, carry):
        feat(raw1m, xm, 1, dx - 4, dx, dx, 0, range(12))
        return carry

    def feat_sides(dx, carry):
        feat(raw1m, xm, 1, dx - 4, dx, dx, 0, range(3))
        feat(raw1m, xm, 1, dx - 4, dx, dx, 288, range(9, 12))
        return carry

    def second(*spans):
        parts = []
        for a in range(3):
            for b in range(3):
                for s in range(3):
                    got = [x[s, od + a, (h + b) * 32 : (h + b + n) * 32, :] for x, od, h, n in spans]
                    parts.append(got[0] if len(got) == 1 else jnp.concatenate(got, axis=0))
        return dot(jnp.concatenate(parts, axis=1), wbig[...])

    def put_keys(raw, od, rows):
        for n, oh in enumerate(rows):
            for c in range(2):
                part = raw[n * 32 : (n + 1) * 32, c * 128 : (c + 1) * 128]
                kf[c, pl.ds(164 + oh * 16 + od, 32, stride=164), :] = part

    def own_second(d2, sums):
        spans = [(x, 2 * d2 + n + first, h, 4) for x, first, h in ((xf, 0, 0), (xm, 3, 3)) for n in range(2)]
        raw = second(*spans)
        for n in range(2):
            d = 2 * d2 + n
            for h in range(4):
                for c in range(2):
                    at = n * 128 + h * 32
                    part = raw[at : at + 32, c * 128 : (c + 1) * 128]
                    ff[c, pl.ds(d * 4 + h, 32, stride=36), :] = part
            put_keys(raw[256 + n * 128 : 384 + n * 128], d + 3, range(3, 7))
        raw_f, raw_m = raw[:256], raw[256:]
        return (
            sums[0] + rows_sum(raw_f),
            sums[1] + rows_sum(raw_f * raw_f),
            sums[2] + rows_sum(raw_m),
            sums[3] + rows_sum(raw_m * raw_m),
        )

    start = tuple(jnp.zeros((8, 256), F32) for _ in range(4))
    sums = lax.fori_loop(0, 4, own_second, start)

    def per_channel_two(s):
        s = jnp.sum(s, axis=0, keepdims=True)
        return s[:, :64] + s[:, 64:128] + s[:, 128:192] + s[:, 192:]

    tile = stat_tile(*[per_channel_two(s) for s in sums])

    def planes(d0, d1):
        def step(od, carry):
            put_keys(second((xm, od, 0, 10)), od, range(10))
            return carry

        lax.fori_loop(d0, d1, step, 0)

    def sides():
        def step(od, carry):
            first = 3 + 2 * od
            raw = second(*[(xm, first + n, h, 3) for n in range(2) for h in (0, 7)])
            for n in range(2):
                put_keys(raw[n * 192 : n * 192 + 192], first + n, (0, 1, 2, 7, 8, 9))
            return carry

        lax.fori_loop(0, 4, step, 0)

    def both_ends():
        lax.fori_loop(0, 3, feat_plane, 0)
        lax.fori_loop(13, 16, feat_plane, 0)
        lax.fori_loop(3, 13, feat_sides, 0)
        planes(0, 3)
        planes(11, 14)

    tile = total_over_devices(
        tile, peers, (ap2, ax2), as2, ar2, (both_ends, sides),
    )
    gain2 = jnp.concatenate([g2[...], g2[...]], axis=1)
    shift2 = jnp.concatenate([s2[...], s2[...]], axis=1)
    pairs2 = scale_and_offset(tile, gain2, shift2)

    def rounded(y):
        return leaky(y).astype(BF16).astype(F32)

    k_i, n_i = iota((512, 128), 0), iota((512, 128), 1)
    hit = jnp.logical_and(n_i < 8, (k_i >> 8) * 2 + ((k_i >> 6) & 1) == (n_i >> 1))
    ones = jnp.where(hit, 1.0, 0.0).astype(BF16)
    row, lane = iota((160, 128), 0), iota((160, 128), 1)
    dd, hh = (row & 15) - (lane - 12), (row >> 4) - (lane - 20)
    bad_d = jnp.logical_and(
        jnp.logical_and(lane >= 12, lane < 20), jnp.logical_or(dd < 0, dd > 6)
    )
    bad_h = jnp.logical_and(
        jnp.logical_and(lane >= 20, lane < 24), jnp.logical_or(hh < 0, hh > 6)
    )
    base = jnp.where(jnp.logical_or(bad_d, bad_h), -BIG, 0.0)
    base = jnp.concatenate([base, base], axis=0)
    lane = iota((320, 128), 1)
    mark = lane - (iota((320, 128), 0) >= 160).astype(I32)
    row = iota((320, 128), 0)
    row = jnp.where(row >= 160, row - 160, row)
    gd, gh = depth * 8 - 3 + (row & 15), height * 4 - 3 + (row >> 4)
    keep = jnp.logical_and(
        jnp.logical_and(gd >= 0, gd < 32), jnp.logical_and(gh >= 0, gh < 128)
    )
    keep = jnp.where(jnp.logical_and(keep, (row & 15) < 14), 1.0, 0.0)
    scale_m, offset_m = pairs2[1][0] * keep, pairs2[1][1] * keep
    odd_lane = (iota((1, 128), 1) & 1) == 1

    def keys(q, carry):
        at = pl.ds(pl.multiple_of(q * 320, 320), 320)
        squares = []
        for c in range(2):
            m = jnp.concatenate([kf[c, pl.ds(q * 328 + n * 164, 160), :] for n in range(2)], axis=0)
            m = leaky(m * scale_m + offset_m).astype(BF16)
            for n in range(2):
                kb[c, pl.ds(pl.multiple_of(q * 320 + n * 160, 160), 160), :] = m[n * 160 : n * 160 + 160]
            m = m.astype(F32)
            sq = m * m
            hi = sq.astype(BF16)
            squares += [hi, (sq - hi.astype(F32)).astype(BF16)]
        norm = dot(jnp.concatenate(squares, axis=1), ones)
        hi = norm.astype(BF16).astype(F32)
        term = norm - jnp.where(odd_lane, hi, 0.0)
        e = jnp.where(mark == 24 + 2 * (q & 1), 1.0, base)
        ke[at, :] = (term + e).astype(BF16)
        return carry

    lax.fori_loop(0, 17, keys, 0)
    for q in (0, 33):
        at = slice(q * 160, q * 160 + 160)
        kb[:, at, :] = jnp.zeros((2, 160, 128), BF16)
        ke[at, :] = jnp.where(lane[:160] == 24 + q % 4, 1.0, base[:160]).astype(BF16)

    rate = sharp[0] * (math.log2(math.e) / 64.0)
    low = iota((32, 128), 1) < 64
    sub = iota((8, 128), 0).astype(F32)
    n_i = iota((1, 128), 1)
    q_w = (n_i >> 5).astype(F32)
    q_d = ((n_i >> 2) & 7).astype(F32)
    q_h = (n_i & 3).astype(F32)
    tiles = [
        [(p, r) for p in range(4) for r in range(4) if -3 <= 4 * (r - 1) + p - 4 * quad <= 6]
        for quad in range(2)
    ]
    zero = jnp.zeros((8, 128), F32)

    def queries(R):
        first, other = [], []
        for quad in range(2):
            at = pl.ds(R * 72 + quad * 36, 32)
            a, b = (
                2.0 * rounded(ff[c, at, :] * pairs2[0][0] + pairs2[0][1]) for c in range(2)
            )
            ra, rb = pltpu.roll(a, 64, 1), pltpu.roll(b, 64, 1)
            first += [jnp.where(low, t, 0.0) for t in (a, ra, b, rb)]
            other += [jnp.where(low, 0.0, t) for t in (ra, a, rb, b)]
        return [jnp.concatenate(t, axis=0).astype(BF16) for t in (first, other)]

    def scores(R, query, phase, buf, best):
        rels = [rel for rel in range(4) if any((phase, rel) in t for t in tiles)]
        count = len(rels) * 160
        rows = pl.ds(pl.multiple_of((2 * R + rels[0]) * 160, 160), count)
        lhs = jnp.concatenate([kb[phase // 2, rows, :], ke[rows, :]], axis=1)
        rhs = jnp.concatenate([query[phase % 2], qe[R & 1, phase]], axis=1)
        score = dot_nt(lhs, rhs)
        for n, rel in enumerate(rels):
            for quad in range(2):
                if (phase, rel) not in tiles[quad]:
                    continue
                place = (quad * 10 + tiles[quad].index((phase, rel))) * 160
                part = score[n * 160 : n * 160 + 160, quad * 128 : quad * 128 + 128]
                buf[place : place + 160, :] = part
                best[quad] = jnp.maximum(best[quad], jnp.max(part.reshape(20, 8, 128), axis=0))

    def weigh(quad, which, buf, top, state):
        for n in which:
            phase, rel = tiles[quad][n]
            tile_sum = zero
            for oh in range(10):
                at_row = (quad * 10 + n) * 160 + oh * 16
                p0 = jnp.exp2(buf[at_row : at_row + 8, :] * rate - top)
                p1 = jnp.exp2(buf[at_row + 8 : at_row + 16, :] * rate - top)
                both = p0 + p1
                state["upper"] = state["upper"] + p1
                state[oh] = state[oh] + both
                tile_sum = tile_sum + both
            state["total"] = state["total"] + tile_sum
            state["w"] = state["w"] + tile_sum * float(4 * (rel - 1) + phase - 4 * quad)

    def finish(R, quad, state):
        h_sum = zero
        for oh in range(1, 10):
            h_sum = h_sum + state[oh] * float(oh)
        d_sum = state["total"] * sub + 8.0 * state["upper"]
        weight = jnp.sum(state["total"], axis=0, keepdims=True)
        for n, (s, own_at) in enumerate(
            ((d_sum, q_d + 3.0), (h_sum, q_h + 3.0), (state["w"], q_w))
        ):
            mean = jnp.sum(s, axis=0, keepdims=True) / weight
            res[n * 2 + quad, pl.ds(R, 1), :] = mean - own_at

    def step(R, buf, best, R_next, buf_next):
        query = queries(R_next)
        best_next = [jnp.full((8, 128), -jnp.inf, F32) for _ in range(2)]
        for quad in range(2):
            top = jnp.max(best[quad], axis=0, keepdims=True) * rate
            top = jnp.broadcast_to(top, (8, 128))
            state = {k: zero for k in list(range(10)) + ["upper", "total", "w"]}
            for half in range(2):
                scores(R_next, query, quad * 2 + half, buf_next, best_next)
                weigh(quad, range(half * 5, half * 5 + 5), buf, top, state)
            finish(R, quad, state)
        return best_next

    def two_blocks(i, best):
        best = step(2 * i, sbuf, list(best), 2 * i + 1, sbuf2)
        best = step(2 * i + 1, sbuf2, best, jnp.minimum(2 * i + 2, 15), sbuf)
        return tuple(best)

    best = [jnp.full((8, 128), -jnp.inf, F32) for _ in range(2)]
    query = queries(0)
    for phase in range(4):
        scores(0, query, phase, sbuf, best)
    lax.fori_loop(0, 8, two_blocks, tuple(best))

    k_i, w_i = iota((128, 128), 0), iota((128, 128), 1)
    order = jnp.where(w_i == (k_i & 15) * 8 + (k_i >> 4), 1.0, 0.0)
    for component in range(3):
        t = [jnp.transpose(res[component * 2 + quad]) for quad in range(2)]
        t = [t[n // 4][(n % 4) * 32 : (n % 4) * 32 + 32] for n in range(8)]
        t = jnp.concatenate(t, axis=1)
        out[component] = jnp.dot(
            t, order, preferred_element_type=F32, precision=lax.Precision.HIGHEST
        )


def local(fi, mi, c1, g1, s1, c2, g2, s2, sharp):
    c1 = jnp.transpose(c1, (2, 3, 4, 1, 0)).reshape(27, 1, 64)
    vec = lambda a: a.reshape(1, 64)
    vmem = pl.BlockSpec(memory_space=pltpu.VMEM)
    tile = lambda n: pltpu.VMEM((n, 2, 128), F32)
    dma = lambda n: pltpu.SemaphoreType.DMA((n,))
    result = pl.pallas_call(
        kernel,
        out_shape=jax.ShapeDtypeStruct((3, 32, 128), F32),
        in_specs=[pl.BlockSpec(memory_space=pl.ANY)] * 8 + [pl.BlockSpec(memory_space=pltpu.SMEM)],
        out_specs=vmem,
        scratch_shapes=[
            pltpu.VMEM((8, 4, 128), F32),
            pltpu.VMEM((8, 4, 128), F32),
            pltpu.VMEM((27, 1, 64), F32),
            pltpu.VMEM((1, 64), F32),
            pltpu.VMEM((1, 64), F32),
            pltpu.VMEM((27, 4096), BF16),
            pltpu.VMEM((1, 64), F32),
            pltpu.VMEM((1, 64), F32),
            pltpu.VMEM((4, 2, 8, 128), F32),
            pltpu.VMEM((14, 2, 24, 128), F32),
            pltpu.VMEM((512, 1024), BF16),
            pltpu.VMEM((27 * 32, 128), F32),
            pltpu.VMEM((3456, 256), BF16),
            pltpu.VMEM((216, 384), BF16),
            pltpu.VMEM((4, 4, 192, 128), F32),
            pltpu.VMEM((3, 4, 192, 384), F32),
            pltpu.VMEM((10, 192, 384), F32),
            pltpu.VMEM((16, 384, 384), F32),
            pltpu.VMEM((3, 10, 192, 128), BF16),
            pltpu.VMEM((3, 16, 384, 128), BF16),
            pltpu.VMEM((2, 32 * 36, 128), F32),
            pltpu.VMEM((2, 34 * 164, 128), F32),
            pltpu.VMEM((2, 34 * 160, 128), BF16),
            pltpu.VMEM((34 * 160, 128), BF16),
            pltpu.VMEM((2, 4, 256, 128), BF16),
            pltpu.VMEM((20 * 160, 128), F32),
            pltpu.VMEM((20 * 160, 128), F32),
            pltpu.VMEM((6, 16, 128), F32),
            tile(16), tile(8), tile(16), tile(8),
            dma(6), dma(6), dma(2), dma(2), dma(2), dma(2), dma(8),
        ],
        compiler_params=pltpu.CompilerParams(
            collective_id=0, has_side_effects=True, vmem_limit_bytes=60 * 1024 * 1024
        ),
    )(fi, mi, c1, vec(g1), vec(s1), c2, vec(g2), vec(s2), sharp)
    return result.reshape(3, 8, 4, 128)


def solution(mesh):
    placed = (P("depth", "height", None),) * 2 + (P(),) * 7
    return jax.shard_map(
        local,
        mesh=mesh,
        in_specs=placed,
        out_specs=P(None, "depth", "height", None),
        check_vma=False,
    )
```

```python
import math

import jax
import jax.numpy as jnp
from jax import lax
from jax.experimental import pallas as pl
from jax.experimental.pallas import tpu as pltpu
from jax.sharding import PartitionSpec as P

MESH = pl.DeviceIdType.MESH
F32, BF16, I32 = jnp.float32, jnp.bfloat16, jnp.int32
BIG = 1e30
CELLS = 32 * 128 * 128
HALO = [(dd, hh) for hh in (-2, -1, 0, 1, 2) for dd in (-1, 0, 1) if (dd, hh) != (0, 0)]
HEIGHT_SPAN = {0: (0, 4, 5), 1: (0, 4, 1), 2: (3, 4, 0), -1: (0, 4, 9), -2: (0, 1, 13)}


def iota(shape, dim):
    return lax.broadcasted_iota(I32, shape, dim)


def dot(a, b):
    return jnp.dot(a, b, preferred_element_type=F32)


def dot_nt(a, b):
    return lax.dot_general(a, b, (((1,), (1,)), ((), ())), preferred_element_type=F32)


def rows_sum(x):
    return jnp.sum(x.reshape(x.shape[0] // 8, 8, x.shape[1]), axis=0)


def position():
    depth, height = lax.axis_index("depth"), lax.axis_index("height")
    return depth, height


def group_peers(depth, height):
    x_hi, zy = height // 16, height % 16
    plane = [(depth, x_hi * 16 + (zy + k) % 16) for k in range(1, 16)]
    along_x = []
    for k in range(1, 8):
        g = (x_hi * 4 + depth + k) % 8
        along_x.append((g % 4, (g // 4) * 16 + zy))
    return plane, along_x


def halo_peers(depth, height):
    return [((depth + dd + 4) % 4, (height + hh + 32) % 32) for dd, hh in HALO]


def total_over_devices(value, peers, bufs, send_sems, recv_sems, works):
    for g, (group, buf, work) in enumerate(zip(peers, bufs, works)):
        buf[0] = value
        for k, peer in enumerate(group):
            pltpu.make_async_remote_copy(
                src_ref=buf.at[0],
                dst_ref=buf.at[k + 1],
                send_sem=send_sems.at[g],
                recv_sem=recv_sems.at[g],
                device_id=peer,
                device_id_type=MESH,
            ).start()
        work()
        tiles = buf.at[pl.ds(1, len(group))]
        pltpu.make_async_copy(tiles, tiles, recv_sems.at[g]).wait()
        pltpu.make_async_copy(tiles, tiles, send_sems.at[g]).wait()
        value = jnp.sum(buf[...], axis=0)
    return value


def leaky(v):
    return jnp.maximum(v, 0.01 * v)


def kernel(
    fi_h, mi_h, c1_h, g1_h, s1_h, c2_h, g2_h, s2_h, sharp,
    out,
    fi, mi, c1, g1, s1, c2, g2, s2,
    own, ext, selm, wf, wbig, w1, v, vs, raw1f, raw1m, xf, xm,
    ff, kf, kb, ke, qe, sbuf, sbuf2, res, ones, kept, window,
    ap1, ax1, ap2, ax2,
    hs, hr, as1, ar1, as2, ar2, ins,
):
    depth, height = position()
    halo = halo_peers(depth, height)
    peers = group_peers(depth, height)

    pairs_in = [(fi_h, fi), (mi_h, mi), (c2_h, c2), (c1_h, c1), (g1_h, g1), (s1_h, s1), (g2_h, g2), (s2_h, s2)]
    loads = [pltpu.make_async_copy(a, b, ins.at[n]) for n, (a, b) in enumerate(pairs_in)]
    for load in loads:
        load.start()
    barrier = pltpu.get_barrier_semaphore()
    everyone = halo + peers[0] + peers[1]
    for peer in everyone:
        pl.semaphore_signal(barrier, inc=1, device_id=peer, device_id_type=MESH)
    loads[0].wait()
    loads[1].wait()
    for h in range(4):
        own[h, 0] = fi[:, h, :]
        own[h, 1] = mi[:, h, :]
    pl.semaphore_wait(barrier, len(everyone))

    copies = []
    for n, (dd, hh) in enumerate(HALO):
        h0, h1, land = HEIGHT_SPAN[hh]
        block = 8 - 8 * dd
        which = {1: 0, -1: 1}.get(dd, 2 + (hh + 2 if hh < 0 else hh + 1))
        copy = pltpu.make_async_remote_copy(
            src_ref=own.at[pl.ds(h0, h1 - h0)],
            dst_ref=ext.at[pl.ds(land, h1 - h0), :, pl.ds(block, 8), :],
            send_sem=hs.at[which],
            recv_sem=hr.at[which],
            device_id=halo[n],
            device_id_type=MESH,
        )
        copy.start()
        if dd == 0:
            copies.append(copy)

    for load in loads[2:]:
        load.wait()
    ext[5:9, :, 8:16, :] = own[...]
    n_i = iota((1, 1024), 1)
    want = 4 * (n_i & 31) - 2 + (n_i >> 7)
    near = jnp.where(iota((128, 1024), 0) == want, 1.0, 0.0)
    for hh in range(4):
        part = jnp.where(((n_i >> 5) & 3) == hh, near, 0.0)
        selm[hh * 128 : (hh + 1) * 128, :] = part.astype(BF16)
    for pair in range(32):
        wf[pl.ds(pair, 27, stride=32), :] = c2[:, pair * 128 : (pair + 1) * 128].astype(F32)

    def build(ab, carry):
        zero = jnp.zeros((64, 64), F32)
        taps = []
        for c in range(3):
            t = wf[pl.ds(pl.multiple_of((ab * 3 + c) * 32, 32), 32), :]
            taps.append(jnp.concatenate([t[:, :64], t[:, 64:]], axis=0))
        for u in range(6):
            parts = [taps[u - wo] if 0 <= u - wo <= 2 else zero for wo in range(4)]
            row = jnp.concatenate(parts, axis=1).astype(BF16)
            wbig[pl.ds(pl.multiple_of((ab * 6 + u) * 64, 64), 64), :] = row
        return carry

    lax.fori_loop(0, 9, build, 0)

    r_i, k_i = iota((64, 64), 0), iota((64, 64), 1)
    even_first = jnp.where(r_i == 2 * (k_i & 31) + (k_i >> 5), 1.0, 0.0)
    c1t = jnp.concatenate([c1[...].reshape(27, 64), jnp.zeros((5, 64), F32)], axis=0)
    c1t = jnp.dot(c1t, even_first, preferred_element_type=F32, precision=lax.Precision.HIGHEST)
    zero = jnp.zeros((32, 64), F32)
    spread = jnp.concatenate(
        [jnp.concatenate([c1t if q == u else zero for q in range(6)], axis=1) for u in range(6)],
        axis=0,
    )
    spread_hi = spread.astype(BF16)
    spread_lo = (spread - spread_hi.astype(F32)).astype(BF16)
    r_i, k_i = iota((72, 192), 0), iota((72, 192), 1)
    tap = k_i % 32
    hit = jnp.logical_and(
        tap // 3 == ((r_i // 8) % 3) * 3 + r_i // 24,
        jnp.logical_and(r_i % 8 - k_i // 32 == tap % 3, tap < 27),
    )
    pick = jnp.where(hit, 1.0, 0.0).astype(BF16)
    w1_hi, w1_lo = dot(pick, spread_hi), dot(pick, spread_lo)
    w1[...] = jnp.concatenate([w1_hi, w1_hi, w1_lo], axis=0).astype(BF16)

    q_i, lane = iota((256, 128), 0), iota((256, 128), 1)
    w_q = q_i >> 5
    e_q = jnp.where(lane - 12 == ((q_i >> 2) & 7), 1.0, 0.0)
    e_q = jnp.where(jnp.logical_and(lane >= 20, lane - 20 == (q_i & 3)), 1.0, e_q)
    lane1 = iota((1, 128), 1)
    in_quad = jnp.logical_and(lane1 >= 24, lane1 < 28)
    for odd in range(2):
        for phase in range(4):
            norm_lane = jnp.logical_and(lane1 < 8, (lane1 >> 1) == phase)
            w_k = 4 * (((lane1 - 24 - 2 * odd + 8) & 3) - 1) + phase
            w_k = jnp.where(in_quad, w_k, w_q)
            e = jnp.where(jnp.abs(w_k - w_q) > 3, -BIG, e_q)
            qe[odd, phase] = jnp.where(norm_lane, -1.0, e).astype(BF16)
    k_i, n_i = iota((512, 128), 0), iota((512, 128), 1)
    hit = jnp.logical_and(n_i < 8, (k_i >> 8) * 2 + ((k_i >> 6) & 1) == (n_i >> 1))
    ones[...] = jnp.where(hit, 1.0, 0.0).astype(BF16)
    row, lane = iota((160, 128), 0), iota((160, 128), 1)
    dd, hh = (row & 15) - (lane - 12), (row >> 4) - (lane - 20)
    bad_d = jnp.logical_and(
        jnp.logical_and(lane >= 12, lane < 20), jnp.logical_or(dd < 0, dd > 6)
    )
    bad_h = jnp.logical_and(
        jnp.logical_and(lane >= 20, lane < 24), jnp.logical_or(hh < 0, hh > 6)
    )
    base = jnp.where(jnp.logical_or(bad_d, bad_h), -BIG, 0.0)
    base = jnp.concatenate([base, base], axis=0)
    lane = iota((320, 128), 1)
    mark = lane - (iota((320, 128), 0) >= 160).astype(I32)
    row = iota((320, 128), 0)
    row = jnp.where(row >= 160, row - 160, row)
    gd, gh = depth * 8 - 3 + (row & 15), height * 4 - 3 + (row >> 4)
    keep = jnp.logical_and(
        jnp.logical_and(gd >= 0, gd < 32), jnp.logical_and(gh >= 0, gh < 128)
    )
    kept[...] = jnp.where(jnp.logical_and(keep, (row & 15) < 14), 1.0, 0.0)
    for odd in range(2):
        window[odd] = jnp.where(mark == 24 + 2 * odd, 1.0, base)

    kf[...] = jnp.zeros_like(kf)

    for copy in copies:
        copy.wait()
    for which, block in ((0, 0), (1, 16)):
        planes_in = ext.at[:, :, pl.ds(block, 8), :]
        pltpu.make_async_copy(planes_in, planes_in, hr.at[which]).wait()
        pltpu.make_async_copy(planes_in, planes_in, hs.at[which]).wait()

    row = iota((48, 128), 0)
    gd = depth * 8 - 8 + row % 24
    d_in = jnp.logical_and(gd >= 0, gd < 32)

    def pick_rows(h4):
        parts = []
        for hh in range(4):
            hx = h4 * 4 + hh
            if hx >= 14:
                parts.append(jnp.zeros((96, 128), BF16))
                continue
            x = ext[hx].reshape(48, 128)
            gh = jnp.full((48, 128), height * 4 - 5 + hx, I32)
            ok = jnp.logical_and(d_in, jnp.logical_and(gh >= 0, gh < 128))
            x = jnp.where(ok, x, 0.0)
            hi = x.astype(BF16)
            lo = (x - hi.astype(F32)).astype(BF16)
            parts.append(jnp.concatenate([hi, lo], axis=0))
        picked = dot(jnp.concatenate(parts, axis=1), selm[...])
        for q in range(4):
            for j in range(8):
                v[q, h4, pl.ds(j, 24, stride=8), :] = picked[
                    q * 24 : q * 24 + 24, j * 128 : (j + 1) * 128
                ]

    def shifted(column, rows):
        for q in range(4):
            full = jnp.concatenate([v[q, column, rows], v[q, column + 1, rows]], axis=1)
            for b in range(3):
                vs[b, q, rows, column * 128 : column * 128 + 128] = full[:, 32 * b : 32 * b + 128]

    own_rows = slice(56, 136)
    pick_rows(1)
    pick_rows(2)
    shifted(1, own_rows)

    def patches(image, dx, lane0, lanes):
        start = pl.multiple_of((dx + 3) * 8, 8)
        parts = [
            vs[b, hl * 2 + image, pl.ds(start, 24), lane0 : lane0 + lanes]
            for hl in (0, 1, 0)
            for b in range(3)
        ]
        return jnp.transpose(jnp.concatenate(parts, axis=0)).astype(BF16)

    def own_sums(dx, sums):
        result = []
        for image in range(2):
            lhs = [patches(image, 4 * dx + n, 128, 128) for n in range(4)]
            raw = dot(jnp.concatenate(lhs, axis=0), w1[...])
            result.append(sums[2 * image] + rows_sum(raw))
            result.append(sums[2 * image + 1] + rows_sum(raw * raw))
        return tuple(result)

    start = tuple(jnp.zeros((8, 384), F32) for _ in range(4))
    sums = lax.fori_loop(1, 3, own_sums, start)

    def per_channel(s):
        s = jnp.sum(s, axis=0, keepdims=True)
        return s[:, 64:128] + s[:, 128:192] + s[:, 192:256] + s[:, 256:320]

    def stat_tile(sum_f, sq_f, sum_m, sq_m):
        return jnp.concatenate(
            [
                jnp.concatenate([sum_f, sum_m], axis=1),
                jnp.concatenate([sq_f, sq_m], axis=1),
            ],
            axis=0,
        )

    tile = stat_tile(*[per_channel(s) for s in sums])

    def raw_fixed():
        def step(dx, carry):
            p = patches(0, dx, 0, 384)
            raw1f[dx - 3] = dot(p[96:288], w1[...])
            return carry

        lax.fori_loop(3, 13, step, 0)

    def raw_moving(d0, d1):
        def step(dx, carry):
            raw1m[dx] = dot(patches(1, dx, 0, 384), w1[...])
            return carry

        lax.fori_loop(d0, d1, step, 0, unroll=2)

    def raw_first():
        pick_rows(0)
        pick_rows(3)
        shifted(1, slice(0, 56))
        shifted(1, slice(136, 192))
        shifted(0, slice(0, 192))
        shifted(2, slice(0, 192))
        raw_fixed()
        raw_moving(0, 8)

    tile = total_over_devices(
        tile, peers, (ap1, ax1), as1, ar1, (raw_first, lambda: raw_moving(8, 16)),
    )

    def scale_and_offset(tile, gain, shift):
        mean = tile[0:1] / CELLS
        mean_sq = tile[1:2] / CELLS
        inv_dev = lax.rsqrt(mean_sq - mean * mean + 1e-05)
        scale = inv_dev * gain
        offset = shift - mean * scale
        pairs = []
        for image in range(2):
            half = slice(image * 64, image * 64 + 64)
            pairs.append(
                tuple(jnp.concatenate([a[:, half], a[:, half]], axis=1) for a in (scale, offset))
            )
        return pairs

    i_i, o_i = iota((64, 128), 0), iota((64, 128), 1) % 64
    perm = jnp.where(i_i == 2 * (o_i % 32) + o_i // 32, 1.0, 0.0)
    gains = jnp.concatenate([g1[...], s1[...], jnp.zeros((6, 64), F32)], axis=0)
    gains = jnp.dot(gains, perm, preferred_element_type=F32, precision=lax.Precision.HIGHEST)
    pairs = scale_and_offset(tile, gains[0:1], gains[1:2])

    def depth_inside(d):
        g = depth * 8 + d
        return jnp.where(jnp.logical_and(g >= 0, g < 32), 1.0, 0.0)

    def height_inside(h):
        g = height * 4 + h
        return jnp.where(jnp.logical_and(g >= 0, g < 128), 1.0, 0.0)

    row, lane = iota((8, 128), 0), iota((8, 128), 1)
    not_before = jnp.logical_or(row > 0, lane >= 64)
    not_after = jnp.logical_or(row < 7, lane < 64)

    def feat(raw, x, image, d, raw_d, x_d, rows, hxs):
        keep_d = depth_inside(d)
        for n, hx in enumerate(hxs):
            keep = keep_d * height_inside(hx - 4)
            scale, offset = pairs[image][0] * keep, pairs[image][1] * keep
            at = slice(rows + n * 32, rows + n * 32 + 32)
            for s in range(3):
                y = leaky(raw[raw_d, at, s * 128 : (s + 1) * 128] * scale + offset)
                if s == 0:
                    y = jnp.concatenate([jnp.where(not_before, y[:8], 0.0), y[8:]], axis=0)
                if s == 2:
                    y = jnp.concatenate([y[:24], jnp.where(not_after, y[24:], 0.0)], axis=0)
                x[s, x_d, at, :] = y.astype(BF16)

    def feat_near(dx, carry):
        feat(raw1f, xf, 0, dx - 4, dx - 3, dx - 3, 0, range(3, 9))
        feat(raw1m, xm, 1, dx - 4, dx, dx, 96, range(3, 9))
        return carry

    lax.fori_loop(3, 13, feat_near, 0)

    def feat_plane(dx, carry):
        feat(raw1m, xm, 1, dx - 4, dx, dx, 0, range(12))
        return carry

    def feat_sides(dx, carry):
        feat(raw1m, xm, 1, dx - 4, dx, dx, 0, range(3))
        feat(raw1m, xm, 1, dx - 4, dx, dx, 288, range(9, 12))
        return carry

    def second(*spans):
        parts = []
        for a in range(3):
            for b in range(3):
                for s in range(3):
                    got = [x[s, od + a, (h + b) * 32 : (h + b + n) * 32, :] for x, od, h, n in spans]
                    parts.append(got[0] if len(got) == 1 else jnp.concatenate(got, axis=0))
        return dot(jnp.concatenate(parts, axis=1), wbig[...])

    def put_keys(raw, od, rows):
        for n, oh in enumerate(rows):
            for c in range(2):
                part = raw[n * 32 : (n + 1) * 32, c * 128 : (c + 1) * 128]
                kf[c, pl.ds(164 + oh * 16 + od, 32, stride=164), :] = part

    def own_second(d2, sums):
        spans = [(x, 2 * d2 + n + first, h, 4) for x, first, h in ((xf, 0, 0), (xm, 3, 3)) for n in range(2)]
        raw = second(*spans)
        for n in range(2):
            d = 2 * d2 + n
            for h in range(4):
                for c in range(2):
                    at = n * 128 + h * 32
                    part = raw[at : at + 32, c * 128 : (c + 1) * 128]
                    ff[c, pl.ds(d * 4 + h, 32, stride=36), :] = part
            put_keys(raw[256 + n * 128 : 384 + n * 128], d + 3, range(3, 7))
        raw_f, raw_m = raw[:256], raw[256:]
        return (
            sums[0] + rows_sum(raw_f),
            sums[1] + rows_sum(raw_f * raw_f),
            sums[2] + rows_sum(raw_m),
            sums[3] + rows_sum(raw_m * raw_m),
        )

    start = tuple(jnp.zeros((8, 256), F32) for _ in range(4))
    sums = lax.fori_loop(0, 4, own_second, start)

    def per_channel_two(s):
        s = jnp.sum(s, axis=0, keepdims=True)
        return s[:, :64] + s[:, 64:128] + s[:, 128:192] + s[:, 192:]

    tile = stat_tile(*[per_channel_two(s) for s in sums])

    def planes(d0, d1):
        def step(od, carry):
            put_keys(second((xm, od, 0, 10)), od, range(10))
            return carry

        lax.fori_loop(d0, d1, step, 0)

    def sides():
        def step(od, carry):
            first = 3 + 2 * od
            raw = second(*[(xm, first + n, h, 3) for n in range(2) for h in (0, 7)])
            for n in range(2):
                put_keys(raw[n * 192 : n * 192 + 192], first + n, (0, 1, 2, 7, 8, 9))
            return carry

        lax.fori_loop(0, 4, step, 0)

    def both_ends():
        lax.fori_loop(0, 3, feat_plane, 0)
        lax.fori_loop(13, 16, feat_plane, 0)
        lax.fori_loop(3, 13, feat_sides, 0)
        planes(0, 3)
        planes(11, 14)

    tile = total_over_devices(
        tile, peers, (ap2, ax2), as2, ar2, (both_ends, sides),
    )
    gain2 = jnp.concatenate([g2[...], g2[...]], axis=1)
    shift2 = jnp.concatenate([s2[...], s2[...]], axis=1)
    pairs2 = scale_and_offset(tile, gain2, shift2)

    def rounded(y):
        return leaky(y).astype(BF16).astype(F32)

    scale_m, offset_m = pairs2[1][0] * kept[...], pairs2[1][1] * kept[...]
    odd_lane = (iota((1, 128), 1) & 1) == 1

    def keys(q, carry):
        at = pl.ds(pl.multiple_of(q * 320, 320), 320)
        squares = []
        for c in range(2):
            m = jnp.concatenate([kf[c, pl.ds(q * 328 + n * 164, 160), :] for n in range(2)], axis=0)
            m = leaky(m * scale_m + offset_m).astype(BF16)
            for n in range(2):
                kb[c, pl.ds(pl.multiple_of(q * 320 + n * 160, 160), 160), :] = m[n * 160 : n * 160 + 160]
            m = m.astype(F32)
            sq = m * m
            hi = sq.astype(BF16)
            squares += [hi, (sq - hi.astype(F32)).astype(BF16)]
        norm = dot(jnp.concatenate(squares, axis=1), ones[...])
        hi = norm.astype(BF16).astype(F32)
        term = norm - jnp.where(odd_lane, hi, 0.0)
        ke[at, :] = (term + window[q & 1]).astype(BF16)
        return carry

    lax.fori_loop(0, 17, keys, 0)
    for q in (0, 33):
        at = slice(q * 160, q * 160 + 160)
        kb[:, at, :] = jnp.zeros((2, 160, 128), BF16)
        ke[at, :] = window[q // 2 % 2, q % 2 * 160 : q % 2 * 160 + 160].astype(BF16)

    rate = sharp[0] * (math.log2(math.e) / 64.0)
    low = iota((32, 128), 1) < 64
    sub = iota((8, 128), 0).astype(F32)
    n_i = iota((1, 128), 1)
    q_w = (n_i >> 5).astype(F32)
    q_d = ((n_i >> 2) & 7).astype(F32)
    q_h = (n_i & 3).astype(F32)
    tiles = [
        [(p, r) for p in range(4) for r in range(4) if -3 <= 4 * (r - 1) + p - 4 * quad <= 6]
        for quad in range(2)
    ]
    zero = jnp.zeros((8, 128), F32)

    def queries(R):
        first, other = [], []
        for quad in range(2):
            at = pl.ds(R * 72 + quad * 36, 32)
            a, b = (
                2.0 * rounded(ff[c, at, :] * pairs2[0][0] + pairs2[0][1]) for c in range(2)
            )
            ra, rb = pltpu.roll(a, 64, 1), pltpu.roll(b, 64, 1)
            first += [jnp.where(low, t, 0.0) for t in (a, ra, b, rb)]
            other += [jnp.where(low, 0.0, t) for t in (ra, a, rb, b)]
        return [jnp.concatenate(t, axis=0).astype(BF16) for t in (first, other)]

    def scores(R, query, phase, buf, best):
        rels = [rel for rel in range(4) if any((phase, rel) in t for t in tiles)]
        count = len(rels) * 160
        rows = pl.ds(pl.multiple_of((2 * R + rels[0]) * 160, 160), count)
        lhs = jnp.concatenate([kb[phase // 2, rows, :], ke[rows, :]], axis=1)
        rhs = jnp.concatenate([query[phase % 2], qe[R & 1, phase]], axis=1)
        score = dot_nt(lhs, rhs)
        for n, rel in enumerate(rels):
            for quad in range(2):
                if (phase, rel) not in tiles[quad]:
                    continue
                place = (quad * 10 + tiles[quad].index((phase, rel))) * 160
                part = score[n * 160 : n * 160 + 160, quad * 128 : quad * 128 + 128]
                buf[place : place + 160, :] = part
                best[quad] = jnp.maximum(best[quad], jnp.max(part.reshape(20, 8, 128), axis=0))

    def weigh(quad, which, buf, top, state):
        for n in which:
            phase, rel = tiles[quad][n]
            tile_sum = zero
            for oh in range(10):
                at_row = (quad * 10 + n) * 160 + oh * 16
                p0 = jnp.exp2(buf[at_row : at_row + 8, :] * rate - top)
                p1 = jnp.exp2(buf[at_row + 8 : at_row + 16, :] * rate - top)
                both = p0 + p1
                state["upper"] = state["upper"] + p1
                state[oh] = state[oh] + both
                tile_sum = tile_sum + both
            state["total"] = state["total"] + tile_sum
            state["w"] = state["w"] + tile_sum * float(4 * (rel - 1) + phase - 4 * quad)

    def finish(R, quad, state):
        h_sum = zero
        for oh in range(1, 10):
            h_sum = h_sum + state[oh] * float(oh)
        d_sum = state["total"] * sub + 8.0 * state["upper"]
        weight = jnp.sum(state["total"], axis=0, keepdims=True)
        for n, (s, own_at) in enumerate(
            ((d_sum, q_d + 3.0), (h_sum, q_h + 3.0), (state["w"], q_w))
        ):
            mean = jnp.sum(s, axis=0, keepdims=True) / weight
            res[n * 2 + quad, pl.ds(R, 1), :] = mean - own_at

    def step(R, buf, best, R_next, buf_next):
        query = queries(R_next)
        best_next = [jnp.full((8, 128), -jnp.inf, F32) for _ in range(2)]
        for quad in range(2):
            top = jnp.max(best[quad], axis=0, keepdims=True) * rate
            top = jnp.broadcast_to(top, (8, 128))
            state = {k: zero for k in list(range(10)) + ["upper", "total", "w"]}
            for half in range(2):
                scores(R_next, query, quad * 2 + half, buf_next, best_next)
                weigh(quad, range(half * 5, half * 5 + 5), buf, top, state)
            finish(R, quad, state)
        return best_next

    def two_blocks(i, best):
        best = step(2 * i, sbuf, list(best), 2 * i + 1, sbuf2)
        best = step(2 * i + 1, sbuf2, best, jnp.minimum(2 * i + 2, 15), sbuf)
        return tuple(best)

    best = [jnp.full((8, 128), -jnp.inf, F32) for _ in range(2)]
    query = queries(0)
    for phase in range(4):
        scores(0, query, phase, sbuf, best)
    lax.fori_loop(0, 8, two_blocks, tuple(best))

    k_i, w_i = iota((128, 128), 0), iota((128, 128), 1)
    order = jnp.where(w_i == (k_i & 15) * 8 + (k_i >> 4), 1.0, 0.0)
    for component in range(3):
        t = [jnp.transpose(res[component * 2 + quad]) for quad in range(2)]
        t = [t[n // 4][(n % 4) * 32 : (n % 4) * 32 + 32] for n in range(8)]
        t = jnp.concatenate(t, axis=1)
        out[component] = jnp.dot(
            t, order, preferred_element_type=F32, precision=lax.Precision.HIGHEST
        )


def local(fi, mi, c1, g1, s1, c2, g2, s2, sharp):
    c1 = jnp.transpose(c1, (2, 3, 4, 1, 0)).reshape(27, 1, 64)
    vec = lambda a: a.reshape(1, 64)
    vmem = pl.BlockSpec(memory_space=pltpu.VMEM)
    tile = lambda n: pltpu.VMEM((n, 2, 128), F32)
    dma = lambda n: pltpu.SemaphoreType.DMA((n,))
    result = pl.pallas_call(
        kernel,
        out_shape=jax.ShapeDtypeStruct((3, 32, 128), F32),
        in_specs=[pl.BlockSpec(memory_space=pl.ANY)] * 8 + [pl.BlockSpec(memory_space=pltpu.SMEM)],
        out_specs=vmem,
        scratch_shapes=[
            pltpu.VMEM((8, 4, 128), F32),
            pltpu.VMEM((8, 4, 128), F32),
            pltpu.VMEM((27, 1, 64), F32),
            pltpu.VMEM((1, 64), F32),
            pltpu.VMEM((1, 64), F32),
            pltpu.VMEM((27, 4096), BF16),
            pltpu.VMEM((1, 64), F32),
            pltpu.VMEM((1, 64), F32),
            pltpu.VMEM((4, 2, 8, 128), F32),
            pltpu.VMEM((14, 2, 24, 128), F32),
            pltpu.VMEM((512, 1024), BF16),
            pltpu.VMEM((27 * 32, 128), F32),
            pltpu.VMEM((3456, 256), BF16),
            pltpu.VMEM((216, 384), BF16),
            pltpu.VMEM((4, 4, 192, 128), F32),
            pltpu.VMEM((3, 4, 192, 384), F32),
            pltpu.VMEM((10, 192, 384), F32),
            pltpu.VMEM((16, 384, 384), F32),
            pltpu.VMEM((3, 10, 192, 128), BF16),
            pltpu.VMEM((3, 16, 384, 128), BF16),
            pltpu.VMEM((2, 32 * 36, 128), F32),
            pltpu.VMEM((2, 34 * 164, 128), F32),
            pltpu.VMEM((2, 34 * 160, 128), BF16),
            pltpu.VMEM((34 * 160, 128), BF16),
            pltpu.VMEM((2, 4, 256, 128), BF16),
            pltpu.VMEM((20 * 160, 128), F32),
            pltpu.VMEM((20 * 160, 128), F32),
            pltpu.VMEM((6, 16, 128), F32),
            pltpu.VMEM((512, 128), BF16),
            pltpu.VMEM((320, 128), F32),
            pltpu.VMEM((2, 320, 128), F32),
            tile(16), tile(8), tile(16), tile(8),
            dma(6), dma(6), dma(2), dma(2), dma(2), dma(2), dma(8),
        ],
        compiler_params=pltpu.CompilerParams(
            collective_id=0, has_side_effects=True, vmem_limit_bytes=60 * 1024 * 1024
        ),
    )(fi, mi, c1, vec(g1), vec(s1), c2, vec(g2), vec(s2), sharp)
    return result.reshape(3, 8, 4, 128)


def solution(mesh):
    placed = (P("depth", "height", None),) * 2 + (P(),) * 7
    return jax.shard_map(
        local,
        mesh=mesh,
        in_specs=placed,
        out_specs=P(None, "depth", "height", None),
        check_vma=False,
    )
```

```python
import math

import jax
import jax.numpy as jnp
from jax import lax
from jax.experimental import pallas as pl
from jax.experimental.pallas import tpu as pltpu
from jax.sharding import PartitionSpec as P

MESH = pl.DeviceIdType.MESH
F32, BF16, I32 = jnp.float32, jnp.bfloat16, jnp.int32
BIG = 1e30
CELLS = 32 * 128 * 128
HALO = [(dd, hh) for hh in (-2, -1, 0, 1, 2) for dd in (-1, 0, 1) if (dd, hh) != (0, 0)]
HEIGHT_SPAN = {0: (0, 4, 5), 1: (0, 4, 1), 2: (3, 4, 0), -1: (0, 4, 9), -2: (0, 1, 13)}


def iota(shape, dim):
    return lax.broadcasted_iota(I32, shape, dim)


def dot(a, b):
    return jnp.dot(a, b, preferred_element_type=F32)


def dot_nt(a, b):
    return lax.dot_general(a, b, (((1,), (1,)), ((), ())), preferred_element_type=F32)


def rows_sum(x):
    return jnp.sum(x.reshape(x.shape[0] // 8, 8, x.shape[1]), axis=0)


def position():
    depth, height = lax.axis_index("depth"), lax.axis_index("height")
    return depth, height


def group_peers(depth, height):
    x_hi, zy = height // 16, height % 16
    plane = [(depth, x_hi * 16 + (zy + k) % 16) for k in range(1, 16)]
    along_x = []
    for k in range(1, 8):
        g = (x_hi * 4 + depth + k) % 8
        along_x.append((g % 4, (g // 4) * 16 + zy))
    return plane, along_x


def halo_peers(depth, height):
    return [((depth + dd + 4) % 4, (height + hh + 32) % 32) for dd, hh in HALO]


def total_over_devices(value, peers, bufs, send_sems, recv_sems, works):
    for g, (group, buf, work) in enumerate(zip(peers, bufs, works)):
        buf[0] = value
        for k, peer in enumerate(group):
            pltpu.make_async_remote_copy(
                src_ref=buf.at[0],
                dst_ref=buf.at[k + 1],
                send_sem=send_sems.at[g],
                recv_sem=recv_sems.at[g],
                device_id=peer,
                device_id_type=MESH,
            ).start()
        work()
        tiles = buf.at[pl.ds(1, len(group))]
        pltpu.make_async_copy(tiles, tiles, recv_sems.at[g]).wait()
        pltpu.make_async_copy(tiles, tiles, send_sems.at[g]).wait()
        value = jnp.sum(buf[...], axis=0)
    return value


def leaky(v):
    return jnp.maximum(v, 0.01 * v)


def kernel(
    fi_h, mi_h, c1_h, g1_h, s1_h, c2_h, g2_h, s2_h, sharp,
    out,
    fi, mi, c1, g1, s1, c2, g2, s2,
    own, ext, selm, wf, wbig, w1, v, vs, raw1f, raw1m, xf, xm,
    ff, kf, kb, ke, qe, sbuf, sbuf2, res, ones, kept, window,
    ap1, ax1, ap2, ax2,
    hs, hr, as1, ar1, as2, ar2, ins,
):
    depth, height = position()
    halo = halo_peers(depth, height)
    peers = group_peers(depth, height)

    pairs_in = [(fi_h, fi), (mi_h, mi), (c2_h, c2), (c1_h, c1), (g1_h, g1), (s1_h, s1), (g2_h, g2), (s2_h, s2)]
    loads = [pltpu.make_async_copy(a, b, ins.at[n]) for n, (a, b) in enumerate(pairs_in)]
    for load in loads:
        load.start()
    barrier = pltpu.get_barrier_semaphore()
    everyone = halo + peers[0] + peers[1]
    for peer in everyone:
        pl.semaphore_signal(barrier, inc=1, device_id=peer, device_id_type=MESH)
    loads[0].wait()
    loads[1].wait()
    for h in range(4):
        own[h, 0] = fi[:, h, :]
        own[h, 1] = mi[:, h, :]
    pl.semaphore_wait(barrier, len(everyone))

    copies = []
    for n, (dd, hh) in enumerate(HALO):
        h0, h1, land = HEIGHT_SPAN[hh]
        block = 8 - 8 * dd
        which = {1: 0, -1: 1}.get(dd, 2 + (hh + 2 if hh < 0 else hh + 1))
        copy = pltpu.make_async_remote_copy(
            src_ref=own.at[pl.ds(h0, h1 - h0)],
            dst_ref=ext.at[pl.ds(land, h1 - h0), :, pl.ds(block, 8), :],
            send_sem=hs.at[which],
            recv_sem=hr.at[which],
            device_id=halo[n],
            device_id_type=MESH,
        )
        copy.start()
        if dd == 0:
            copies.append(copy)

    for load in loads[2:]:
        load.wait()
    ext[5:9, :, 8:16, :] = own[...]
    n_i = iota((1, 1024), 1)
    want = 4 * (n_i & 31) - 2 + (n_i >> 7)
    near = jnp.where(iota((128, 1024), 0) == want, 1.0, 0.0)
    for hh in range(4):
        part = jnp.where(((n_i >> 5) & 3) == hh, near, 0.0)
        selm[hh * 128 : (hh + 1) * 128, :] = part.astype(BF16)
    for pair in range(32):
        wf[pl.ds(pair, 27, stride=32), :] = c2[:, pair * 128 : (pair + 1) * 128].astype(F32)

    def build(ab, carry):
        zero = jnp.zeros((64, 64), F32)
        taps = []
        for c in range(3):
            t = wf[pl.ds(pl.multiple_of((ab * 3 + c) * 32, 32), 32), :]
            taps.append(jnp.concatenate([t[:, :64], t[:, 64:]], axis=0))
        for u in range(6):
            parts = [taps[u - wo] if 0 <= u - wo <= 2 else zero for wo in range(4)]
            row = jnp.concatenate(parts, axis=1).astype(BF16)
            wbig[pl.ds(pl.multiple_of((ab * 6 + u) * 64, 64), 64), :] = row
        return carry

    lax.fori_loop(0, 9, build, 0)

    r_i, k_i = iota((64, 64), 0), iota((64, 64), 1)
    even_first = jnp.where(r_i == 2 * (k_i & 31) + (k_i >> 5), 1.0, 0.0)
    c1t = jnp.concatenate([c1[...].reshape(27, 64), jnp.zeros((5, 64), F32)], axis=0)
    c1t = jnp.dot(c1t, even_first, preferred_element_type=F32, precision=lax.Precision.HIGHEST)
    zero = jnp.zeros((32, 64), F32)
    spread = jnp.concatenate(
        [jnp.concatenate([c1t if q == u else zero for q in range(6)], axis=1) for u in range(6)],
        axis=0,
    )
    spread_hi = spread.astype(BF16)
    spread_lo = (spread - spread_hi.astype(F32)).astype(BF16)
    r_i, k_i = iota((72, 192), 0), iota((72, 192), 1)
    tap = k_i % 32
    hit = jnp.logical_and(
        tap // 3 == ((r_i // 8) % 3) * 3 + r_i // 24,
        jnp.logical_and(r_i % 8 - k_i // 32 == tap % 3, tap < 27),
    )
    pick = jnp.where(hit, 1.0, 0.0).astype(BF16)
    w1_hi, w1_lo = dot(pick, spread_hi), dot(pick, spread_lo)
    w1[...] = jnp.concatenate([w1_hi, w1_hi, w1_lo], axis=0).astype(BF16)

    q_i, lane = iota((256, 128), 0), iota((256, 128), 1)
    w_q = q_i >> 5
    e_q = jnp.where(lane - 12 == ((q_i >> 2) & 7), 1.0, 0.0)
    e_q = jnp.where(jnp.logical_and(lane >= 20, lane - 20 == (q_i & 3)), 1.0, e_q)
    lane1 = iota((1, 128), 1)
    in_quad = jnp.logical_and(lane1 >= 24, lane1 < 28)
    for odd in range(2):
        for phase in range(4):
            norm_lane = jnp.logical_and(lane1 < 8, (lane1 >> 1) == phase)
            w_k = 4 * (((lane1 - 24 - 2 * odd + 8) & 3) - 1) + phase
            w_k = jnp.where(in_quad, w_k, w_q)
            e = jnp.where(jnp.abs(w_k - w_q) > 3, -BIG, e_q)
            qe[odd, phase] = jnp.where(norm_lane, -1.0, e).astype(BF16)
    k_i, n_i = iota((512, 128), 0), iota((512, 128), 1)
    hit = jnp.logical_and(n_i < 8, (k_i >> 8) * 2 + ((k_i >> 6) & 1) == (n_i >> 1))
    ones[...] = jnp.where(hit, 1.0, 0.0).astype(BF16)
    row, lane = iota((160, 128), 0), iota((160, 128), 1)
    dd, hh = (row & 15) - (lane - 12), (row >> 4) - (lane - 20)
    bad_d = jnp.logical_and(
        jnp.logical_and(lane >= 12, lane < 20), jnp.logical_or(dd < 0, dd > 6)
    )
    bad_h = jnp.logical_and(
        jnp.logical_and(lane >= 20, lane < 24), jnp.logical_or(hh < 0, hh > 6)
    )
    base = jnp.where(jnp.logical_or(bad_d, bad_h), -BIG, 0.0)
    base = jnp.concatenate([base, base], axis=0)
    lane = iota((320, 128), 1)
    mark = lane - (iota((320, 128), 0) >= 160).astype(I32)
    row = iota((320, 128), 0)
    row = jnp.where(row >= 160, row - 160, row)
    gd, gh = depth * 8 - 3 + (row & 15), height * 4 - 3 + (row >> 4)
    keep = jnp.logical_and(
        jnp.logical_and(gd >= 0, gd < 32), jnp.logical_and(gh >= 0, gh < 128)
    )
    kept[...] = jnp.where(jnp.logical_and(keep, (row & 15) < 14), 1.0, 0.0)
    for odd in range(2):
        window[odd] = jnp.where(mark == 24 + 2 * odd, 1.0, base)

    kf[...] = jnp.zeros_like(kf)

    for copy in copies:
        copy.wait()
    for which, block in ((0, 0), (1, 16)):
        planes_in = ext.at[:, :, pl.ds(block, 8), :]
        pltpu.make_async_copy(planes_in, planes_in, hr.at[which]).wait()
        pltpu.make_async_copy(planes_in, planes_in, hs.at[which]).wait()

    row = iota((48, 128), 0)
    gd = depth * 8 - 8 + row % 24
    d_in = jnp.logical_and(gd >= 0, gd < 32)

    def pick_rows(h4):
        parts = []
        for hh in range(4):
            hx = h4 * 4 + hh
            if hx >= 14:
                parts.append(jnp.zeros((96, 128), BF16))
                continue
            x = ext[hx].reshape(48, 128)
            gh = jnp.full((48, 128), height * 4 - 5 + hx, I32)
            ok = jnp.logical_and(d_in, jnp.logical_and(gh >= 0, gh < 128))
            x = jnp.where(ok, x, 0.0)
            hi = x.astype(BF16)
            lo = (x - hi.astype(F32)).astype(BF16)
            parts.append(jnp.concatenate([hi, lo], axis=0))
        picked = dot(jnp.concatenate(parts, axis=1), selm[...])
        for q in range(4):
            for j in range(8):
                v[q, h4, pl.ds(j, 24, stride=8), :] = picked[
                    q * 24 : q * 24 + 24, j * 128 : (j + 1) * 128
                ]

    def shifted(column, rows):
        for q in range(4):
            full = jnp.concatenate([v[q, column, rows], v[q, column + 1, rows]], axis=1)
            for b in range(3):
                vs[b, q, rows, column * 128 : column * 128 + 128] = full[:, 32 * b : 32 * b + 128]

    own_rows = slice(56, 136)
    pick_rows(1)
    pick_rows(2)
    shifted(1, own_rows)

    def patches(image, dx, lane0, lanes):
        start = pl.multiple_of((dx + 3) * 8, 8)
        parts = [
            vs[b, hl * 2 + image, pl.ds(start, 24), lane0 : lane0 + lanes]
            for hl in (0, 1, 0)
            for b in range(3)
        ]
        return jnp.transpose(jnp.concatenate(parts, axis=0)).astype(BF16)

    def own_sums(dx, sums):
        result = []
        for image in range(2):
            lhs = [patches(image, 4 * dx + n, 128, 128) for n in range(4)]
            raw = dot(jnp.concatenate(lhs, axis=0), w1[...])
            result.append(sums[2 * image] + rows_sum(raw))
            result.append(sums[2 * image + 1] + rows_sum(raw * raw))
        return tuple(result)

    start = tuple(jnp.zeros((8, 384), F32) for _ in range(4))
    sums = lax.fori_loop(1, 3, own_sums, start)

    def per_channel(s):
        s = jnp.sum(s, axis=0, keepdims=True)
        return s[:, 64:128] + s[:, 128:192] + s[:, 192:256] + s[:, 256:320]

    def stat_tile(sum_f, sq_f, sum_m, sq_m):
        return jnp.concatenate(
            [
                jnp.concatenate([sum_f, sum_m], axis=1),
                jnp.concatenate([sq_f, sq_m], axis=1),
            ],
            axis=0,
        )

    tile = stat_tile(*[per_channel(s) for s in sums])

    def raw_fixed():
        def step(dx, carry):
            p = patches(0, dx, 0, 384)
            raw1f[dx - 3] = dot(p[96:288], w1[...])
            return carry

        lax.fori_loop(3, 13, step, 0, unroll=2)

    def raw_moving(d0, d1):
        def step(dx, carry):
            raw1m[dx] = dot(patches(1, dx, 0, 384), w1[...])
            return carry

        lax.fori_loop(d0, d1, step, 0, unroll=2)

    def raw_first():
        pick_rows(0)
        pick_rows(3)
        shifted(1, slice(0, 56))
        shifted(1, slice(136, 192))
        shifted(0, slice(0, 192))
        shifted(2, slice(0, 192))
        raw_fixed()
        raw_moving(0, 8)

    tile = total_over_devices(
        tile, peers, (ap1, ax1), as1, ar1, (raw_first, lambda: raw_moving(8, 16)),
    )

    def scale_and_offset(tile, gain, shift):
        mean = tile[0:1] / CELLS
        mean_sq = tile[1:2] / CELLS
        inv_dev = lax.rsqrt(mean_sq - mean * mean + 1e-05)
        scale = inv_dev * gain
        offset = shift - mean * scale
        pairs = []
        for image in range(2):
            half = slice(image * 64, image * 64 + 64)
            pairs.append(
                tuple(jnp.concatenate([a[:, half], a[:, half]], axis=1) for a in (scale, offset))
            )
        return pairs

    i_i, o_i = iota((64, 128), 0), iota((64, 128), 1) % 64
    perm = jnp.where(i_i == 2 * (o_i % 32) + o_i // 32, 1.0, 0.0)
    gains = jnp.concatenate([g1[...], s1[...], jnp.zeros((6, 64), F32)], axis=0)
    gains = jnp.dot(gains, perm, preferred_element_type=F32, precision=lax.Precision.HIGHEST)
    pairs = scale_and_offset(tile, gains[0:1], gains[1:2])

    def depth_inside(d):
        g = depth * 8 + d
        return jnp.where(jnp.logical_and(g >= 0, g < 32), 1.0, 0.0)

    def height_inside(h):
        g = height * 4 + h
        return jnp.where(jnp.logical_and(g >= 0, g < 128), 1.0, 0.0)

    row, lane = iota((8, 128), 0), iota((8, 128), 1)
    not_before = jnp.logical_or(row > 0, lane >= 64)
    not_after = jnp.logical_or(row < 7, lane < 64)

    def feat(raw, x, image, d, raw_d, x_d, rows, hxs):
        keep_d = depth_inside(d)
        for n, hx in enumerate(hxs):
            keep = keep_d * height_inside(hx - 4)
            scale, offset = pairs[image][0] * keep, pairs[image][1] * keep
            at = slice(rows + n * 32, rows + n * 32 + 32)
            for s in range(3):
                y = leaky(raw[raw_d, at, s * 128 : (s + 1) * 128] * scale + offset)
                if s == 0:
                    y = jnp.concatenate([jnp.where(not_before, y[:8], 0.0), y[8:]], axis=0)
                if s == 2:
                    y = jnp.concatenate([y[:24], jnp.where(not_after, y[24:], 0.0)], axis=0)
                x[s, x_d, at, :] = y.astype(BF16)

    def feat_near(dx, carry):
        feat(raw1f, xf, 0, dx - 4, dx - 3, dx - 3, 0, range(3, 9))
        feat(raw1m, xm, 1, dx - 4, dx, dx, 96, range(3, 9))
        return carry

    lax.fori_loop(3, 13, feat_near, 0, unroll=2)

    def feat_plane(dx, carry):
        feat(raw1m, xm, 1, dx - 4, dx, dx, 0, range(12))
        return carry

    def feat_sides(dx, carry):
        feat(raw1m, xm, 1, dx - 4, dx, dx, 0, range(3))
        feat(raw1m, xm, 1, dx - 4, dx, dx, 288, range(9, 12))
        return carry

    def second(*spans):
        parts = []
        for a in range(3):
            for b in range(3):
                for s in range(3):
                    got = [x[s, od + a, (h + b) * 32 : (h + b + n) * 32, :] for x, od, h, n in spans]
                    parts.append(got[0] if len(got) == 1 else jnp.concatenate(got, axis=0))
        return dot(jnp.concatenate(parts, axis=1), wbig[...])

    def put_keys(raw, od, rows):
        for n, oh in enumerate(rows):
            for c in range(2):
                part = raw[n * 32 : (n + 1) * 32, c * 128 : (c + 1) * 128]
                kf[c, pl.ds(164 + oh * 16 + od, 32, stride=164), :] = part

    def own_second(d2, sums):
        spans = [(x, 2 * d2 + n + first, h, 4) for x, first, h in ((xf, 0, 0), (xm, 3, 3)) for n in range(2)]
        raw = second(*spans)
        for n in range(2):
            d = 2 * d2 + n
            for h in range(4):
                for c in range(2):
                    at = n * 128 + h * 32
                    part = raw[at : at + 32, c * 128 : (c + 1) * 128]
                    ff[c, pl.ds(d * 4 + h, 32, stride=36), :] = part
            put_keys(raw[256 + n * 128 : 384 + n * 128], d + 3, range(3, 7))
        raw_f, raw_m = raw[:256], raw[256:]
        return (
            sums[0] + rows_sum(raw_f),
            sums[1] + rows_sum(raw_f * raw_f),
            sums[2] + rows_sum(raw_m),
            sums[3] + rows_sum(raw_m * raw_m),
        )

    start = tuple(jnp.zeros((8, 256), F32) for _ in range(4))
    sums = lax.fori_loop(0, 4, own_second, start)

    def per_channel_two(s):
        s = jnp.sum(s, axis=0, keepdims=True)
        return s[:, :64] + s[:, 64:128] + s[:, 128:192] + s[:, 192:]

    tile = stat_tile(*[per_channel_two(s) for s in sums])

    def planes(d0, d1):
        def step(od, carry):
            put_keys(second((xm, od, 0, 10)), od, range(10))
            return carry

        lax.fori_loop(d0, d1, step, 0)

    def sides():
        def step(od, carry):
            first = 3 + 2 * od
            raw = second(*[(xm, first + n, h, 3) for n in range(2) for h in (0, 7)])
            for n in range(2):
                put_keys(raw[n * 192 : n * 192 + 192], first + n, (0, 1, 2, 7, 8, 9))
            return carry

        lax.fori_loop(0, 4, step, 0)

    def both_ends():
        lax.fori_loop(0, 3, feat_plane, 0)
        lax.fori_loop(13, 16, feat_plane, 0)
        lax.fori_loop(3, 13, feat_sides, 0, unroll=2)
        planes(0, 3)
        planes(11, 14)

    tile = total_over_devices(
        tile, peers, (ap2, ax2), as2, ar2, (both_ends, sides),
    )
    gain2 = jnp.concatenate([g2[...], g2[...]], axis=1)
    shift2 = jnp.concatenate([s2[...], s2[...]], axis=1)
    pairs2 = scale_and_offset(tile, gain2, shift2)

    def rounded(y):
        return leaky(y).astype(BF16).astype(F32)

    scale_m, offset_m = pairs2[1][0] * kept[...], pairs2[1][1] * kept[...]
    odd_lane = (iota((1, 128), 1) & 1) == 1

    def keys(q, carry):
        at = pl.ds(pl.multiple_of(q * 320, 320), 320)
        squares = []
        for c in range(2):
            m = jnp.concatenate([kf[c, pl.ds(q * 328 + n * 164, 160), :] for n in range(2)], axis=0)
            m = leaky(m * scale_m + offset_m).astype(BF16)
            for n in range(2):
                kb[c, pl.ds(pl.multiple_of(q * 320 + n * 160, 160), 160), :] = m[n * 160 : n * 160 + 160]
            m = m.astype(F32)
            sq = m * m
            hi = sq.astype(BF16)
            squares += [hi, (sq - hi.astype(F32)).astype(BF16)]
        norm = dot(jnp.concatenate(squares, axis=1), ones[...])
        hi = norm.astype(BF16).astype(F32)
        term = norm - jnp.where(odd_lane, hi, 0.0)
        ke[at, :] = (term + window[q & 1]).astype(BF16)
        return carry

    lax.fori_loop(0, 17, keys, 0)
    for q in (0, 33):
        at = slice(q * 160, q * 160 + 160)
        kb[:, at, :] = jnp.zeros((2, 160, 128), BF16)
        ke[at, :] = window[q // 2 % 2, q % 2 * 160 : q % 2 * 160 + 160].astype(BF16)

    rate = sharp[0] * (math.log2(math.e) / 64.0)
    low = iota((32, 128), 1) < 64
    sub = iota((8, 128), 0).astype(F32)
    n_i = iota((1, 128), 1)
    q_w = (n_i >> 5).astype(F32)
    q_d = ((n_i >> 2) & 7).astype(F32)
    q_h = (n_i & 3).astype(F32)
    tiles = [
        [(p, r) for p in range(4) for r in range(4) if -3 <= 4 * (r - 1) + p - 4 * quad <= 6]
        for quad in range(2)
    ]
    zero = jnp.zeros((8, 128), F32)

    def queries(R):
        first, other = [], []
        for quad in range(2):
            at = pl.ds(R * 72 + quad * 36, 32)
            a, b = (
                2.0 * rounded(ff[c, at, :] * pairs2[0][0] + pairs2[0][1]) for c in range(2)
            )
            ra, rb = pltpu.roll(a, 64, 1), pltpu.roll(b, 64, 1)
            first += [jnp.where(low, t, 0.0) for t in (a, ra, b, rb)]
            other += [jnp.where(low, 0.0, t) for t in (ra, a, rb, b)]
        return [jnp.concatenate(t, axis=0).astype(BF16) for t in (first, other)]

    def scores(R, query, phase, buf, best):
        rels = [rel for rel in range(4) if any((phase, rel) in t for t in tiles)]
        count = len(rels) * 160
        rows = pl.ds(pl.multiple_of((2 * R + rels[0]) * 160, 160), count)
        lhs = jnp.concatenate([kb[phase // 2, rows, :], ke[rows, :]], axis=1)
        rhs = jnp.concatenate([query[phase % 2], qe[R & 1, phase]], axis=1)
        score = dot_nt(lhs, rhs)
        for n, rel in enumerate(rels):
            for quad in range(2):
                if (phase, rel) not in tiles[quad]:
                    continue
                place = (quad * 10 + tiles[quad].index((phase, rel))) * 160
                part = score[n * 160 : n * 160 + 160, quad * 128 : quad * 128 + 128]
                buf[place : place + 160, :] = part
                best[quad] = jnp.maximum(best[quad], jnp.max(part.reshape(20, 8, 128), axis=0))

    def weigh(quad, which, buf, top, state):
        for n in which:
            phase, rel = tiles[quad][n]
            tile_sum = zero
            for oh in range(10):
                at_row = (quad * 10 + n) * 160 + oh * 16
                p0 = jnp.exp2(buf[at_row : at_row + 8, :] * rate - top)
                p1 = jnp.exp2(buf[at_row + 8 : at_row + 16, :] * rate - top)
                both = p0 + p1
                state["upper"] = state["upper"] + p1
                state[oh] = state[oh] + both
                tile_sum = tile_sum + both
            state["total"] = state["total"] + tile_sum
            state["w"] = state["w"] + tile_sum * float(4 * (rel - 1) + phase - 4 * quad)

    def finish(R, quad, state):
        h_sum = zero
        for oh in range(1, 10):
            h_sum = h_sum + state[oh] * float(oh)
        d_sum = state["total"] * sub + 8.0 * state["upper"]
        weight = jnp.sum(state["total"], axis=0, keepdims=True)
        for n, (s, own_at) in enumerate(
            ((d_sum, q_d + 3.0), (h_sum, q_h + 3.0), (state["w"], q_w))
        ):
            mean = jnp.sum(s, axis=0, keepdims=True) / weight
            res[n * 2 + quad, pl.ds(R, 1), :] = mean - own_at

    def step(R, buf, best, R_next, buf_next):
        query = queries(R_next)
        best_next = [jnp.full((8, 128), -jnp.inf, F32) for _ in range(2)]
        for quad in range(2):
            top = jnp.max(best[quad], axis=0, keepdims=True) * rate
            top = jnp.broadcast_to(top, (8, 128))
            state = {k: zero for k in list(range(10)) + ["upper", "total", "w"]}
            for half in range(2):
                scores(R_next, query, quad * 2 + half, buf_next, best_next)
                weigh(quad, range(half * 5, half * 5 + 5), buf, top, state)
            finish(R, quad, state)
        return best_next

    def two_blocks(i, best):
        best = step(2 * i, sbuf, list(best), 2 * i + 1, sbuf2)
        best = step(2 * i + 1, sbuf2, best, jnp.minimum(2 * i + 2, 15), sbuf)
        return tuple(best)

    best = [jnp.full((8, 128), -jnp.inf, F32) for _ in range(2)]
    query = queries(0)
    for phase in range(4):
        scores(0, query, phase, sbuf, best)
    lax.fori_loop(0, 8, two_blocks, tuple(best))

    k_i, w_i = iota((128, 128), 0), iota((128, 128), 1)
    order = jnp.where(w_i == (k_i & 15) * 8 + (k_i >> 4), 1.0, 0.0)
    for component in range(3):
        t = [jnp.transpose(res[component * 2 + quad]) for quad in range(2)]
        t = [t[n // 4][(n % 4) * 32 : (n % 4) * 32 + 32] for n in range(8)]
        t = jnp.concatenate(t, axis=1)
        out[component] = jnp.dot(
            t, order, preferred_element_type=F32, precision=lax.Precision.HIGHEST
        )


def local(fi, mi, c1, g1, s1, c2, g2, s2, sharp):
    c1 = jnp.transpose(c1, (2, 3, 4, 1, 0)).reshape(27, 1, 64)
    vec = lambda a: a.reshape(1, 64)
    vmem = pl.BlockSpec(memory_space=pltpu.VMEM)
    tile = lambda n: pltpu.VMEM((n, 2, 128), F32)
    dma = lambda n: pltpu.SemaphoreType.DMA((n,))
    result = pl.pallas_call(
        kernel,
        out_shape=jax.ShapeDtypeStruct((3, 32, 128), F32),
        in_specs=[pl.BlockSpec(memory_space=pl.ANY)] * 8 + [pl.BlockSpec(memory_space=pltpu.SMEM)],
        out_specs=vmem,
        scratch_shapes=[
            pltpu.VMEM((8, 4, 128), F32),
            pltpu.VMEM((8, 4, 128), F32),
            pltpu.VMEM((27, 1, 64), F32),
            pltpu.VMEM((1, 64), F32),
            pltpu.VMEM((1, 64), F32),
            pltpu.VMEM((27, 4096), BF16),
            pltpu.VMEM((1, 64), F32),
            pltpu.VMEM((1, 64), F32),
            pltpu.VMEM((4, 2, 8, 128), F32),
            pltpu.VMEM((14, 2, 24, 128), F32),
            pltpu.VMEM((512, 1024), BF16),
            pltpu.VMEM((27 * 32, 128), F32),
            pltpu.VMEM((3456, 256), BF16),
            pltpu.VMEM((216, 384), BF16),
            pltpu.VMEM((4, 4, 192, 128), F32),
            pltpu.VMEM((3, 4, 192, 384), F32),
            pltpu.VMEM((10, 192, 384), F32),
            pltpu.VMEM((16, 384, 384), F32),
            pltpu.VMEM((3, 10, 192, 128), BF16),
            pltpu.VMEM((3, 16, 384, 128), BF16),
            pltpu.VMEM((2, 32 * 36, 128), F32),
            pltpu.VMEM((2, 34 * 164, 128), F32),
            pltpu.VMEM((2, 34 * 160, 128), BF16),
            pltpu.VMEM((34 * 160, 128), BF16),
            pltpu.VMEM((2, 4, 256, 128), BF16),
            pltpu.VMEM((20 * 160, 128), F32),
            pltpu.VMEM((20 * 160, 128), F32),
            pltpu.VMEM((6, 16, 128), F32),
            pltpu.VMEM((512, 128), BF16),
            pltpu.VMEM((320, 128), F32),
            pltpu.VMEM((2, 320, 128), F32),
            tile(16), tile(8), tile(16), tile(8),
            dma(6), dma(6), dma(2), dma(2), dma(2), dma(2), dma(8),
        ],
        compiler_params=pltpu.CompilerParams(
            collective_id=0, has_side_effects=True, vmem_limit_bytes=60 * 1024 * 1024
        ),
    )(fi, mi, c1, vec(g1), vec(s1), c2, vec(g2), vec(s2), sharp)
    return result.reshape(3, 8, 4, 128)


def solution(mesh):
    placed = (P("depth", "height", None),) * 2 + (P(),) * 7
    return jax.shard_map(
        local,
        mesh=mesh,
        in_specs=placed,
        out_specs=P(None, "depth", "height", None),
        check_vma=False,
    )
```
